256 devices in a mesh: grp: 16 (over x, y), seq: 16 (over z, core).
Axes of the slice: x: 4, y: 4, z: 8, core: 2. Of those that a mesh axis runs over, the one named last changes fastest.
Arguments:
- query_input: bfloat16 [32768, 4096], P(('grp', 'seq')), may hold values from -8 to 8
- key_input: bfloat16 [32768, 512], P(('grp', 'seq')), may hold values from -8 to 8
- value_input: bfloat16 [32768, 512], P(('grp', 'seq')), may hold values from -6 to 6
- out_grad: bfloat16 [32768, 4096], P(('grp', 'seq')), may hold values from -6 to 6
- key_blocks: int32 [256, 12], replicated, may hold values from 0 to 255, as said below
- key_counts: int32 [256], replicated, may hold values from 1 to 12, as said below
- block_position: int32 [256], replicated, may hold values from 0 to 255, each once
Outputs:
- attn_out: bfloat16 [32768, 4096], P(('grp', 'seq'))
- query_grad: bfloat16 [32768, 4096], P(('grp', 'seq'))
- key_grad: bfloat16 [32768, 512], P(('grp', 'seq'))
- value_grad: bfloat16 [32768, 512], P(('grp', 'seq'))
The draws below stay inside these ranges and needn't reach their ends.
Inputs may be any that keep to these rules, and one draw needn't show every extreme that they name: `key_blocks`: in row b the first key_counts[b] entries are distinct, the first is b itself and the others are earlier blocks of the same group of 16 blocks or of the group before; the remaining entries equal b. `key_counts`: the last block's count is 12.
All inputs are finite; a program needn't handle non-finite values.
Results may differ from the reference program's by a relative error of at most 0.015.
Values may be sent and summed in bfloat16 or wider, within the bound.
A program may use at most 128 MiB of HBM per device.

```python
import math
import jax
import jax.numpy as jnp
from jax import lax

HEADS = 32
KV_HEADS = 4
HEAD_DIM = 128
BLK = 128
KB = 12
GB = 16
NB = 256
TOKENS = 32768


def mask_tables(key):
    block_ids = jnp.arange(NB, dtype=jnp.int32)
    group_ids = block_ids // GB
    lowest = jnp.maximum(group_ids - 1, 0) * GB
    reachable = block_ids - lowest + 1
    drawn_counts = jax.random.randint(jax.random.fold_in(key, 11), (NB,), 1, KB + 1, dtype=jnp.int32)
    counts = jnp.minimum(drawn_counts, reachable)
    counts = jnp.where(block_ids == NB - 1, KB, counts).astype(jnp.int32)
    window_size = 2 * GB - 1
    offsets = jnp.arange(1, window_size + 1, dtype=jnp.int32)
    random_part = jax.random.randint(jax.random.fold_in(key, 12), (NB, window_size), 0, 2 ** 20, dtype=jnp.int32)
    candidates = block_ids[:, None] - offsets[None, :]
    scores = jnp.where(candidates >= lowest[:, None], random_part * window_size + offsets[None, :], -offsets[None, :])
    top_scores, picked = lax.top_k(scores, KB - 1)
    chosen = block_ids[:, None] - (picked.astype(jnp.int32) + 1)
    listed = jnp.concatenate([block_ids[:, None], chosen], axis=1)
    slot_ids = jnp.arange(KB, dtype=jnp.int32)
    listed = jnp.where(slot_ids[None, :] < counts[:, None], listed, block_ids[:, None])
    return (listed.astype(jnp.int32), counts)


def draw_key_blocks(key, part):
    return mask_tables(key)[0]


def draw_key_counts(key, part):
    return mask_tables(key)[1]


def drawn_fields(key):
    head_ratio = HEADS // KV_HEADS
    base_query = jnp.clip(jax.random.normal(jax.random.fold_in(key, 21), (TOKENS, KV_HEADS, head_ratio, HEAD_DIM), jnp.float32), -6.0, 6.0)
    base_key = jnp.clip(jax.random.normal(jax.random.fold_in(key, 22), (TOKENS, KV_HEADS, HEAD_DIM), jnp.float32), -6.0, 6.0)
    return (base_query.reshape(TOKENS, HEADS * HEAD_DIM), base_key.reshape(TOKENS, KV_HEADS * HEAD_DIM))


def draw_query_input(key, part):
    return drawn_fields(key)[0].astype(jnp.bfloat16)


def draw_key_input(key, part):
    return drawn_fields(key)[1].astype(jnp.bfloat16)


def block_scale(key, extent, shards, smallest, largest):
    gain = 1.0
    for dim, blocks in shards:
        steps = jax.random.uniform(jax.random.fold_in(jax.random.fold_in(key, 6), dim), (blocks,), jnp.float32, smallest / len(shards), largest / len(shards))
        gain = gain * jnp.repeat(jnp.exp(steps), extent[dim] // blocks).reshape((-1,) + (1,) * (len(extent) - 1 - dim))
    return gain


def bell_draw(key, extent, deviation, bound, cuts=(), kind=jnp.bfloat16):
    entries = deviation * jax.random.normal(key, extent, jnp.float32)
    if cuts:
        entries = entries * block_scale(key, extent, cuts, -0.22, 0.18)
    return jnp.clip(entries, -bound, bound).astype(kind)


def setup_inputs(seed: int = 0) -> dict:
    seeds = jax.random.split(jax.random.key(seed), 8)
    return {
        "query_input": draw_query_input(jax.random.fold_in(seeds[7], 71), 0),
        "key_input": draw_key_input(jax.random.fold_in(seeds[7], 71), 0),
        "value_input": bell_draw(seeds[2], (TOKENS, KV_HEADS * HEAD_DIM), 1.0, 6.0, ((0, 256),)),
        "out_grad": bell_draw(seeds[3], (TOKENS, HEADS * HEAD_DIM), 1.0, 6.0, ((0, 256),)),
        "key_blocks": draw_key_blocks(jax.random.fold_in(seeds[7], 71), 0),
        "key_counts": draw_key_counts(jax.random.fold_in(seeds[7], 71), 0),
        "block_position": jax.random.permutation(seeds[6], NB).astype(jnp.int32),
    }


def rope_tables(places):
    offsets = jnp.arange(BLK, dtype=jnp.int32)
    positions = (places[:, None] * BLK + offsets[None, :]).astype(jnp.float32)
    exponents = jnp.arange(HEAD_DIM // 2, dtype=jnp.float32) * (2.0 / HEAD_DIM)
    frequency = jnp.power(jnp.float32(500000.0), -exponents)
    angles = positions[:, :, None] * frequency
    return (jnp.cos(angles), jnp.sin(angles))

def rotate(values, cosine, sine_part):
    half_dim = HEAD_DIM // 2
    first_half = values[..., :half_dim]
    second_half = values[..., half_dim:]
    return jnp.concatenate([first_half * cosine - second_half * sine_part, second_half * cosine + first_half * sine_part], axis=-1)

def unrotate(values, cosine, sine_part):
    half_dim = HEAD_DIM // 2
    first_half = values[..., :half_dim]
    second_half = values[..., half_dim:]
    return jnp.concatenate([first_half * cosine + second_half * sine_part, second_half * cosine - first_half * sine_part], axis=-1)

def reference(query_input, key_input, value_input, out_grad, key_blocks, key_counts, block_position):
    head_ratio = HEADS // KV_HEADS
    score_scale = 1.0 / math.sqrt(HEAD_DIM)
    cosine, sine_part = rope_tables(block_position)
    query_cos = cosine[:, :, None, None, :]
    query_sin = sine_part[:, :, None, None, :]
    key_cos = cosine[:, :, None, :]
    key_sin = sine_part[:, :, None, :]
    q_rot = rotate(query_input.astype(jnp.float32).reshape(NB, BLK, KV_HEADS, head_ratio, HEAD_DIM), query_cos, query_sin).astype(jnp.bfloat16)
    k_rot = rotate(key_input.astype(jnp.float32).reshape(NB, BLK, KV_HEADS, HEAD_DIM), key_cos, key_sin).astype(jnp.bfloat16)
    value_blocks = value_input.reshape(NB, BLK, KV_HEADS, HEAD_DIM)
    grad_blocks = out_grad.reshape(NB, BLK, KV_HEADS, head_ratio, HEAD_DIM)
    offsets = jnp.arange(BLK, dtype=jnp.int32)
    causal_lower = offsets[None, :] <= offsets[:, None]
    slot_ids = jnp.arange(KB, dtype=jnp.int32)

    def advance(running, block_id):
        key_acc, value_acc = running
        listed = key_blocks[block_id]
        usable = slot_ids < key_counts[block_id]
        diagonal_hit = listed == block_id
        allowed = usable[None, :, None] & (jnp.logical_not(diagonal_hit)[None, :, None] | causal_lower[:, None, :])
        query_here = q_rot[block_id].astype(jnp.float32)
        key_here = k_rot[listed].astype(jnp.float32)
        value_here = value_blocks[listed].astype(jnp.float32)
        grad_here = grad_blocks[block_id].astype(jnp.float32)
        scores = jnp.einsum('tgrd,jugd->grtju', query_here, key_here) * score_scale
        scores = jnp.where(allowed[None, None], scores, -jnp.inf)
        row_max = lax.optimization_barrier(jnp.max(scores, axis=(3, 4), keepdims=True))
        weights = jnp.exp(scores - row_max)
        probs_full = weights / lax.optimization_barrier(jnp.sum(weights, axis=(3, 4), keepdims=True))
        probs_low = lax.optimization_barrier(probs_full.astype(jnp.bfloat16)).astype(jnp.float32)
        attended = lax.optimization_barrier(jnp.einsum('grtju,jugd->tgrd', probs_low, value_here).astype(jnp.bfloat16))
        row_delta = lax.optimization_barrier(jnp.sum(grad_here * attended.astype(jnp.float32), axis=-1))
        dprobs = jnp.einsum('tgrd,jugd->grtju', grad_here, value_here)
        dscores = probs_full * (dprobs - jnp.transpose(row_delta, (1, 2, 0))[:, :, :, None, None])
        dscores_low = lax.optimization_barrier(dscores.astype(jnp.bfloat16)).astype(jnp.float32)
        query_part = (jnp.einsum('grtju,jugd->tgrd', dscores_low, key_here) * score_scale).astype(jnp.bfloat16)
        key_part = jnp.einsum('grtju,tgrd->jugd', dscores_low, query_here) * score_scale
        value_part = jnp.einsum('grtju,tgrd->jugd', probs_low, grad_here)
        key_acc = key_acc.at[listed].add(key_part)
        value_acc = value_acc.at[listed].add(value_part)
        return ((key_acc, value_acc), (attended, query_part))
    zero_grads = jnp.zeros((NB, BLK, KV_HEADS, HEAD_DIM), jnp.float32)
    (key_acc, value_acc), (out_blocks, dq_blocks) = lax.scan(advance, (zero_grads, zero_grads), jnp.arange(NB, dtype=jnp.int32))
    attn_out = out_blocks.reshape(TOKENS, HEADS * HEAD_DIM)
    query_grad = unrotate(dq_blocks.astype(jnp.float32), query_cos, query_sin).astype(jnp.bfloat16).reshape(TOKENS, HEADS * HEAD_DIM)
    key_grad = unrotate(key_acc, key_cos, key_sin).astype(jnp.bfloat16).reshape(TOKENS, KV_HEADS * HEAD_DIM)
    value_grad = value_acc.astype(jnp.bfloat16).reshape(TOKENS, KV_HEADS * HEAD_DIM)
    return (attn_out, query_grad, key_grad, value_grad)
```

```python
import functools
import math

import jax
import jax.numpy as jnp
from jax import lax
from jax.experimental import pallas as pl
from jax.experimental.pallas import tpu as pltpu
from jax.sharding import PartitionSpec as P

HEADS = 32
KV_HEADS = 4
D = 128
BLK = 128
KB = 12
GB = 16
NK = KB * BLK
HALF = HEADS * D // 2
QW = 8 * D
ROWS = 512
MESH = pl.DeviceIdType.MESH
BF = jnp.bfloat16
F32 = jnp.float32
LOG2E = 1.0 / math.log(2.0)
SCALE = 1.0 / math.sqrt(D)


def nt(a, b):
    return lax.dot_general(a, b, (((1,), (1,)), ((), ())), preferred_element_type=F32)


def nn(a, b):
    return lax.dot_general(a, b, (((1,), (0,)), ((), ())), preferred_element_type=F32)


def kernel(
    n_grp,
    n_z,
    reach,
    kb_ref,
    kc_ref,
    q_ref,
    k_ref,
    v_ref,
    do_ref,
    cos_ref,
    sin_ref,
    out_ref,
    qg_ref,
    kgr_ref,
    vgr_ref,
    kv0,
    kv1,
    pt0,
    pt1,
    rb0,
    rb1,
    sb0,
    sb1,
    ks,
    q_own,
    q_send,
    q_par,
    do_par,
    o_scr,
    dq_scr,
    py_s,
    py_r,
    fo,
    f_s,
    f_r,
    kg,
    vg,
    s_scr,
    e_scr,
    ds_scr,
    q_t,
    do_t,
    inv,
    ss_kv,
    sr_kv,
    ss_x,
    sr_x,
    ss_ag,
    sr_ag,
    ss_ay,
    sr_ay,
    ss_rs,
    sr_rs,
    ss_ry,
    sr_ry,
    ss_f,
    sr_f,
    ss_o,
    sr_o,
):
    kvs, pts, rbs, sbs = (kv0, kv1), (pt0, pt1), (rb0, rb1), (sb0, sb1)
    g = lax.axis_index("grp")
    s_id = lax.axis_index("seq")
    z = s_id // 2
    c = s_id % 2
    other = 1 - c

    def at_z(off):
        return lax.rem(z + off + 2 * n_z, n_z)

    def dev(dg=0, dz=0, flip=False):
        core = other if flip else c
        return {"grp": lax.rem(g + dg + n_grp, n_grp), "seq": at_z(dz) * 2 + core}

    def copy(src, dst, ss, sr, to):
        return pltpu.make_async_remote_copy(
            src_ref=src, dst_ref=dst, send_sem=ss, recv_sem=sr, device_id=to, device_id_type=MESH
        )

    sends = []

    def start(d):
        d.start()
        sends.append(d)

    barrier = pltpu.get_barrier_semaphore()
    peers = [dev(flip=True), dev(dz=1), dev(dz=-1), dev(dg=1), dev(dg=-1)]
    for p in peers:
        pl.semaphore_signal(barrier, inc=1, device_id=p, device_id_type=MESH)

    def cols(base, width=D):
        return pl.ds(pl.multiple_of(base, D), width)

    cos_own, sin_own = cos_ref[1], sin_ref[1]

    def rot(x, cs, sn):
        return x * cs + pltpu.roll(x, D // 2, 1) * sn

    my_slot = GB + 2 * z + c
    for u in range(2):
        for mine in (False, True):
            h = (c if mine else other) * 2 + u
            kr = rot(k_ref[:, cols(h * D)].astype(F32), cos_own, sin_own).astype(BF)
            if mine:
                kvs[u][my_slot, 0] = kr
                kvs[u][my_slot, 1] = v_ref[:, cols(h * D)]
            else:
                ks[u, 0] = kr
                ks[u, 1] = v_ref[:, cols(h * D)]
    pl.semaphore_wait(barrier, len(peers))

    def kv_chip(u):
        return copy(ks.at[u], kvs[u].at[my_slot], ss_kv.at[u], sr_kv.at[u], dev(flip=True))

    def kv_chip_in(u):
        return copy(
            ks.at[u], kvs[u].at[GB + 2 * z + other], ss_kv.at[u], sr_kv.at[u], dev(flip=True)
        )

    def do_copy(u):
        return copy(
            do_ref.at[:, cols(other * HALF + u * QW, QW)],
            do_par.at[:, u * QW : (u + 1) * QW],
            ss_x.at[0, u],
            sr_x.at[0, u],
            dev(flip=True),
        )

    def q_copy(u):
        return copy(
            q_send.at[:, u * QW : (u + 1) * QW],
            q_par.at[:, u * QW : (u + 1) * QW],
            ss_x.at[1, u],
            sr_x.at[1, u],
            dev(flip=True),
        )

    start(kv_chip(0))
    start(kv_chip(1))

    def piece(u, grp, zc, dr, d):
        base = grp * GB + 2 * zc
        if d == n_z // 2:
            return kvs[u].at[pl.ds(base + dr, 1)]
        return kvs[u].at[pl.ds(base, 2)]

    far = n_z // 2

    def ag_out(u, grp, dr, d):
        step = 1 if dr == 0 else -1
        zc = at_z(-step * (d - 1))
        p = piece(u, grp, zc, dr, d)
        return copy(p, p, ss_ag.at[u, grp, dr, d - 1], sr_ag.at[u, grp, dr, d - 1], dev(dz=step))

    def ag_in(u, grp, dr, d):
        step = 1 if dr == 0 else -1
        p = piece(u, grp, at_z(-step * d), dr, d)
        return copy(p, p, ss_ag.at[u, grp, dr, d - 1], sr_ag.at[u, grp, dr, d - 1], dev(dz=step))

    def ay(u, k):
        zc = at_z(k)
        return copy(
            kvs[u].at[pl.ds(GB + 2 * zc, 2)],
            kvs[u].at[pl.ds(2 * zc, 2)],
            ss_ay.at[u, k + 2],
            sr_ay.at[u, k + 2],
            dev(dg=1),
        )

    def ag(u, s):
        if s == 0:
            kv_chip_in(u).wait_recv()
            start(ay(u, 0))
            start(ag_out(u, 1, 0, 1))
            start(ag_out(u, 1, 1, 1))
            return
        k = s - 1
        if k == 0:
            ay(u, 0).wait_recv()
            if reach < 1:
                start(ag_out(u, 0, 0, 1))
                start(ag_out(u, 0, 1, 1))
        else:
            for dr, sign in ((0, -1), (1, 1)):
                if k <= reach:
                    ay(u, sign * k).wait_recv()
                else:
                    ag_in(u, 0, dr, k).wait_recv()
                if k + 1 > reach and k < far:
                    start(ag_out(u, 0, dr, k + 1))
        if s <= far:
            for dr, sign in ((0, -1), (1, 1)):
                ag_in(u, 1, dr, s).wait_recv()
                if s < far:
                    start(ag_out(u, 1, dr, s + 1))
                if s <= reach:
                    start(ay(u, sign * s))

    def q_rope(u):
        for mine in (False, True):
            base = (c if mine else other) * HALF + u * QW
            dst = q_own if mine else q_send
            for h in range(8):
                x = q_ref[:, cols(base + h * D)].astype(F32)
                x = rot(x, cos_own, sin_own) * (SCALE * LOG2E)
                dst[:, u * QW + h * D : u * QW + (h + 1) * D] = x.astype(BF)
            if not mine:
                start(q_copy(u))
                start(do_copy(u))

    row0 = g * GB + 2 * z
    first = (g - 1) * GB
    rows = (row0 + other, row0 + c)

    def invert(kb, carry):
        for b in range(2):
            found = jnp.int32(KB)
            for j in range(KB):
                hit = (kb_ref[rows[b], j] - first == kb) & (j < kc_ref[rows[b]])
                found = jnp.where(hit, j, found)
            inv[b, kb] = found
        return carry

    rr = lax.broadcasted_iota(jnp.int32, (ROWS, BLK), 0) & (BLK - 1)
    cc = lax.broadcasted_iota(jnp.int32, (ROWS, BLK), 1)
    KW = 256

    def gather(u, b):
        for j in range(KB):
            i = jnp.clip(kb_ref[rows[b], j] - first, 0, 2 * GB - 1)
            kg[j * BLK : (j + 1) * BLK, :] = kvs[u][i, 0]
            vg[j * BLK : (j + 1) * BLK, 0:D] = kvs[u][i, 1]

    def compute(u, b, half):
        count = kc_ref[rows[b]]
        r = slice(half * ROWS, (half + 1) * ROWS)
        heads = [half * 4 + x for x in range(4)]
        src_q = q_par if b == 0 else q_own
        q = jnp.concatenate(
            [src_q[:, u * QW + h * D : u * QW + (h + 1) * D] for h in heads], axis=0
        )
        q_t[:, r] = q.T
        mx = None
        for n in range(NK // KW):
            s = nt(q, kg[n * KW : (n + 1) * KW, :])
            for t in range(KW // BLK):
                j = n * (KW // BLK) + t
                st = s[:, t * BLK : (t + 1) * BLK]
                if j == 0:
                    st = jnp.where((cc <= rr) & (j < count), st, -1e30)
                else:
                    st = jnp.where(j < count, st, -1e30)
                s_scr[:, j * BLK : (j + 1) * BLK] = st
                mx = st if mx is None else jnp.maximum(mx, st)
        m = jnp.max(mx, axis=1, keepdims=True)
        for j in range(KB):
            ks_ = slice(j * BLK, (j + 1) * BLK)
            e_scr[r, ks_] = jnp.exp2(s_scr[:, ks_] - m).astype(BF)
        ox = nn(e_scr[r, :], vg[...])
        norm = 1.0 / ox[:, D:]
        o = ox[:, :D] * norm
        if b == 0:
            gr = jnp.concatenate(
                [do_par[:, u * QW + h * D : u * QW + (h + 1) * D] for h in heads], axis=0
            )
        else:
            gr = jnp.concatenate(
                [do_ref[:, cols(c * HALF + u * QW + h * D)] for h in heads], axis=0
            )
        gs = (gr.astype(F32) * norm).astype(BF)
        do_t[:, r] = gs.T
        delta = jnp.sum(gs.astype(F32) * o, axis=1, keepdims=True)
        for n in range(NK // KW):
            ks_ = slice(n * KW, (n + 1) * KW)
            dp = nt(gs, vg[ks_, 0:D])
            ds_scr[r, ks_] = (e_scr[r, ks_].astype(F32) * (dp - delta)).astype(BF)
        dq = nn(ds_scr[r, :], kg[...])
        cs, sn = cos_ref[b] * SCALE, sin_ref[b] * -SCALE
        for x, h in enumerate(heads):
            oh = o[x * BLK : (x + 1) * BLK].astype(BF)
            dh = rot(dq[x * BLK : (x + 1) * BLK], cs, sn).astype(BF)
            if b == 0:
                at = slice(u * QW + h * D, u * QW + (h + 1) * D)
                o_scr[:, at] = oh
                dq_scr[:, at] = dh
            else:
                at = cols(c * HALF + u * QW + h * D)
                out_ref[:, at] = oh
                qg_ref[:, at] = dh

    def o_copy(u, which):
        src, dst = ((o_scr, out_ref), (dq_scr, qg_ref))[which]
        return copy(
            src.at[:, u * QW : (u + 1) * QW],
            dst.at[:, cols(c * HALF + u * QW, QW)],
            ss_o.at[u, which],
            sr_o.at[u, which],
            dev(flip=True),
        )

    def o_copy_in(u, which):
        src, dst = ((o_scr, out_ref), (dq_scr, qg_ref))[which]
        return copy(
            src.at[:, u * QW : (u + 1) * QW],
            dst.at[:, cols(other * HALF + u * QW, QW)],
            ss_o.at[u, which],
            sr_o.at[u, which],
            dev(flip=True),
        )

    def key_grads(u, b):
        if b == 0:
            start(o_copy(u, 0))
            start(o_copy(u, 1))
        for n in range(NK // KW):
            ks_ = slice(n * KW, (n + 1) * KW)
            dv = nn(do_t[...], e_scr[:, ks_])
            dk = nn(q_t[...], ds_scr[:, ks_])
            for t in range(KW // BLK):
                j = n * (KW // BLK) + t
                pts[u][b, j, 0] = dk[:, t * BLK : (t + 1) * BLK].astype(BF)
                pts[u][b, j, 1] = dv[:, t * BLK : (t + 1) * BLK].astype(BF)

    def term(u, slot, w):
        a = pts[u][0, inv[0, slot], w].astype(F32)
        return a + pts[u][1, inv[1, slot], w].astype(F32)

    def rs_out(u, grp, dr, s):
        step = 1 if dr == 0 else -1
        to = dev(dz=step)
        sems = (ss_rs.at[u, grp, dr, s], sr_rs.at[u, grp, dr, s])
        if s == 0:
            return copy(sbs[u].at[grp, dr], rbs[u].at[grp, dr, 0, dr], *sems, to)
        return copy(rbs[u].at[grp, dr, s - 1], rbs[u].at[grp, dr, s], *sems, to)

    def rs(u, s):
        if s == 0:
            for grp in (0, 1):
                for dr in (0, 1):
                    slot = grp * GB + 2 * at_z(far) + dr
                    for w in (0, 1):
                        sbs[u][grp, dr, w] = term(u, slot, w).astype(BF)
                    start(rs_out(u, grp, dr, 0))
        elif s < far:
            for grp in (0, 1):
                for dr in (0, 1):
                    step = 1 if dr == 0 else -1
                    rs_out(u, grp, dr, s - 1).wait_recv()
                    base = grp * GB + 2 * at_z(step * (far - s))
                    for blk in (0, 1):
                        for w in (0, 1):
                            x = term(u, base + blk, w)
                            if s > 1 or blk == dr:
                                x = x + rbs[u][grp, dr, s - 1, blk, w].astype(F32)
                            rbs[u][grp, dr, s - 1, blk, w] = x.astype(BF)
                    start(rs_out(u, grp, dr, s))
        elif s == far:
            for grp in (0, 1):
                for dr in (0, 1):
                    rs_out(u, grp, dr, s - 1).wait_recv()
                base = grp * GB + 2 * z
                for blk in (0, 1):
                    for w in (0, 1):
                        x = term(u, base + blk, w)
                        x = x + rbs[u][grp, 0, far - 1, blk, w].astype(F32)
                        x = x + rbs[u][grp, 1, far - 1, blk, w].astype(F32)
                        if grp == 0:
                            py_s[u, blk, w] = x.astype(BF)
                        else:
                            fo[u, blk, w] = x
                if grp == 0:
                    start(py(u))
        elif s == far + 1:
            py(u).wait_recv()
            for w in (0, 1):
                f_s[u, w] = fo[u, other, w] + py_r[u, other, w].astype(F32)
            start(f_copy(u))
            for w in (0, 1):
                finish(u, c, w, fo[u, c, w] + py_r[u, c, w].astype(F32))
        else:
            f_copy(u).wait_recv()
            for w in (0, 1):
                finish(u, other, w, f_r[u, w])

    def py(u):
        return copy(py_s.at[u], py_r.at[u], ss_ry.at[u], sr_ry.at[u], dev(dg=-1))

    def f_copy(u):
        return copy(f_s.at[u], f_r.at[u], ss_f.at[u], sr_f.at[u], dev(flip=True))

    def finish(u, core, w, x):
        at = cols((core * 2 + u) * D)
        x = x.T
        if w == 0:
            x = rot(x * (1.0 / LOG2E), cos_own, -sin_own)
            kgr_ref[:, at] = x.astype(BF)
        else:
            vgr_ref[:, at] = x.astype(BF)

    def x_wait(u):
        q_copy(u).wait_recv()
        do_copy(u).wait_recv()

    ag(0, 0)
    q_rope(0)
    vg[:, D:] = jnp.ones((NK, D), BF)
    for u in range(2):
        for b in range(2):
            for w in range(2):
                pts[u][b, KB, w] = jnp.zeros((D, BLK), BF)
    lax.fori_loop(0, 2 * GB, invert, 0)
    ag(0, 1)
    q_rope(1)
    ag(0, 2)
    ag(0, 3)
    ag(1, 0)
    ag(0, 4)
    ag(0, 5)
    x_wait(0)
    gather(0, 0)
    compute(0, 0, 0)
    ag(1, 1)
    compute(0, 0, 1)
    key_grads(0, 0)
    ag(1, 2)
    gather(0, 1)
    compute(0, 1, 0)
    ag(1, 3)
    compute(0, 1, 1)
    key_grads(0, 1)
    ag(1, 4)
    rs(0, 0)
    ag(1, 5)
    x_wait(1)
    gather(1, 0)
    compute(1, 0, 0)
    rs(0, 1)
    compute(1, 0, 1)
    key_grads(1, 0)
    rs(0, 2)
    gather(1, 1)
    compute(1, 1, 0)
    rs(0, 3)
    compute(1, 1, 1)
    key_grads(1, 1)
    rs(1, 0)
    rs(0, 4)
    rs(1, 1)
    rs(0, 5)
    rs(1, 2)
    rs(0, 6)
    rs(1, 3)
    rs(1, 4)
    rs(1, 5)
    for u in range(2):
        for which in range(2):
            o_copy_in(u, which).wait_recv()
    rs(1, 6)
    for d in sends:
        d.wait_send()


def local(n_grp, n_seq, q, k, v, do, key_blocks, key_counts, block_position):
    n_z = n_seq // 2
    far = n_z // 2
    me = lax.axis_index("grp") * n_seq + lax.axis_index("seq")
    core = lax.axis_index("seq") % 2
    pair = lax.dynamic_slice_in_dim(block_position, me - core, 2, 0)
    places = jnp.where(core == 0, pair[::-1], pair)
    offsets = jnp.arange(BLK, dtype=jnp.int32)
    positions = (places[:, None] * BLK + offsets[None, :]).astype(F32)
    exponents = jnp.arange(D // 2, dtype=F32) * (2.0 / D)
    frequency = jnp.power(F32(500000.0), -exponents)
    angles = positions[:, :, None] * frequency
    cosine, sine = jnp.cos(angles), jnp.sin(angles)
    cos2 = jnp.concatenate([cosine, cosine], axis=-1)
    sin2 = jnp.concatenate([-sine, sine], axis=-1)
    vm = pl.BlockSpec(memory_space=pltpu.VMEM)
    sm = pl.BlockSpec(memory_space=pltpu.SMEM)
    dma = pltpu.SemaphoreType.DMA
    tok = q.shape[0]
    nslot = 2 * GB
    V = pltpu.VMEM
    scratch = [
        V((nslot, 2, BLK, D), BF),
        V((nslot, 2, BLK, D), BF),
        V((2, KB + 1, 2, D, BLK), BF),
        V((2, KB + 1, 2, D, BLK), BF),
        V((2, 2, far, 2, 2, D, BLK), BF),
        V((2, 2, far, 2, 2, D, BLK), BF),
        V((2, 2, 2, D, BLK), BF),
        V((2, 2, 2, D, BLK), BF),
        V((2, 2, BLK, D), BF),
        V((tok, HALF), BF),
        V((tok, HALF), BF),
        V((tok, HALF), BF),
        V((tok, HALF), BF),
        V((tok, HALF), BF),
        V((tok, HALF), BF),
        V((2, 2, 2, D, BLK), BF),
        V((2, 2, 2, D, BLK), BF),
        V((2, 2, 2, D, BLK), F32),
        V((2, 2, D, BLK), F32),
        V((2, 2, D, BLK), F32),
        V((NK, D), BF),
        V((NK, 2 * D), BF),
        V((ROWS, NK), F32),
        V((8 * BLK, NK), BF),
        V((8 * BLK, NK), BF),
        V((D, 8 * BLK), BF),
        V((D, 8 * BLK), BF),
        pltpu.SMEM((2, nslot), jnp.int32),
    ]
    for shape in (
        (2,),
        (2, 2),
        (2, 2, 2, far),
        (2, 5),
        (2, 2, 2, far),
        (2,),
        (2,),
        (2, 2),
    ):
        scratch += [dma(shape), dma(shape)]
    return pl.pallas_call(
        functools.partial(kernel, n_grp, n_z, 0),
        out_shape=[
            jax.ShapeDtypeStruct(q.shape, BF),
            jax.ShapeDtypeStruct(q.shape, BF),
            jax.ShapeDtypeStruct(k.shape, BF),
            jax.ShapeDtypeStruct(k.shape, BF),
        ],
        in_specs=[sm, sm] + [vm] * 6,
        out_specs=[vm] * 4,
        scratch_shapes=scratch,
        compiler_params=pltpu.CompilerParams(
            collective_id=0, has_side_effects=True, vmem_limit_bytes=60 * 2**20
        ),
    )(key_blocks, key_counts, q, k, v, do, cos2, sin2)


def solution(mesh):
    rows = P(("grp", "seq"), None)
    return jax.shard_map(
        functools.partial(local, mesh.shape["grp"], mesh.shape["seq"]),
        mesh=mesh,
        in_specs=(rows, rows, rows, rows, P(), P(), P()),
        out_specs=(rows, rows, rows, rows),
        check_vma=False,
    )
```

```python
import functools
import math

import jax
import jax.numpy as jnp
import numpy as np
from jax import lax
from jax.experimental import pallas as pl
from jax.experimental.pallas import tpu as pltpu
from jax.sharding import PartitionSpec as P

HEADS = 32
KV_HEADS = 4
D = 128
BLK = 128
KB = 12
GB = 16
NK = KB * BLK
HALF = HEADS * D // 2
QW = 8 * D
KW = 256
ROWS = 512
MESH = pl.DeviceIdType.MESH
BF = jnp.bfloat16
F32 = jnp.float32
LOG2E = 1.0 / math.log(2.0)
SCALE = 1.0 / math.sqrt(D)
PIECES = 30
FREQ = np.tile(500000.0 ** (-np.arange(D // 2) / (D // 2)), 2).astype(np.float32)[None]
FAR = 4
REACH = 2
REACH_R = 2
ORDER = (
    0, 1500000, 1400000, 100, 1600000, 1410000, 1510000, 1000, 300000, 100001, 100011, 300100,
    100101, 100111, 1100, 301000, 101001, 101011, 200001, 100002, 100012, 200011, 100102, 100112,
    200101, 101101, 101111, 200111, 101002, 101012, 301100, 100003, 100013, 201001, 201011,
    100103, 100113, 200002, 101102, 101112, 200012, 101003, 101013, 200102, 10000, 100004, 200112,
    201101, 100114, 200003, 201111, 101113, 101103, 201002, 10100, 200013, 101004, 201012, 110011,
    200103, 201102, 200113, 110001, 201112, 11000, 200004, 101114, 310000, 201003, 110111, 310100,
    110101, 201013, 210011, 11100, 201103, 110012, 210001, 110002, 200114, 901000, 201113, 311000,
    111001, 901100, 201004, 210101, 210111, 110102, 111011, 900000, 110112, 311100, 111101,
    111111, 900100, 210012, 210002, 110003, 110013, 201114, 1001000, 211001, 111002, 1001100,
    210102, 110103, 111012, 1000000, 110113, 211011, 111102, 1000100, 210112, 111112, 1301000,
    210003, 210013, 211101, 1300000, 110004, 501001, 501004, 501011, 501013, 501101, 501103,
    501111, 501114, 401004, 401013, 401103, 401114, 601000, 601100, 211002, 211111, 111003,
    111013, 1101000, 210103, 110114, 211012, 210113, 211102, 111103, 1101100, 210004, 211112,
    111113, 1100000, 501003, 501012, 501102, 501113, 1100100, 401003, 401113, 1201000, 211003,
    211013, 1200000, 210114, 111004, 500001, 500004, 500011, 500013, 500101, 211103, 500103,
    211113, 500111, 500114, 400004, 400013, 400103, 400114, 600000, 401012, 600100, 911000,
    501002, 501112, 401102, 111114, 911100, 211004, 910000, 500003, 500012, 910100, 211114,
    500102, 1011000, 500113, 400003, 1011100, 401101, 400113, 1010000, 401011, 500002, 1010100,
    401002, 1311000, 401112, 1310000, 500112, 400012, 511001, 511004, 511011, 511013, 400102,
    511101, 511103, 511111, 511114, 411004, 411013, 411103, 411114, 611000, 611100, 1111000,
    400002, 401001, 1111100, 401111, 1110000, 400011, 400101, 400112, 511003, 511012, 511113,
    1110100, 511102, 411003, 1211000, 411113, 701100, 400001, 1210000, 701000, 510001, 510004,
    510011, 510013, 510101, 510103, 510111, 510114, 410004, 410013, 410103, 411012, 410114,
    610000, 610100, 400111, 511002, 511112, 411102, 801100, 700000, 801000, 510003, 510012,
    510102, 510113, 410003, 800000, 411011, 411101, 410113, 510002, 700100, 411002, 510112,
    411112, 410012, 410102, 800100, 410002, 411001, 410112, 411111, 410011, 410101, 410001,
    711000, 410111, 711100, 710000, 811000, 710100, 811100, 810000, 810100,
)


def nt(a, b):
    return lax.dot_general(a, b, (((1,), (1,)), ((), ())), preferred_element_type=F32)


def nn(a, b):
    return lax.dot_general(a, b, (((1,), (0,)), ((), ())), preferred_element_type=F32)


def far_of(dr, pb):
    return FAR if dr == pb else FAR - 1


def kernel(n_grp, n_z, reach, reach_r, *refs):
    (
        hbm_in,
        (out_ref, qg_ref, kgr_ref, vgr_ref),
        kvs,
        pts,
        rbs,
        (ks, q_own, q_send, q_par, do_par, o_scr, dq_scr),
        (sb, yb, f_s, f_r),
        (kb_ref, kc_ref, bp_ref, fr_ref, q_ref, k_ref, v_ref, do_ref, cos_ref, sin_ref),
        (kg, vg, s_scr, e_scr, ds_scr, q_t, do_t, g_scr, dl_scr, inv),
        sems,
    ) = split(refs)
    kvs = (kvs[0:2], kvs[2:4])
    pts = (pts[0:2], pts[2:4])
    rbs = (rbs[0:2], rbs[2:4])
    in_sem, ring_sem, ag_sem, rs_sem = sems[:4]
    kv_sem, x_sem, f_sem, o_sem = [sems[4 + 2 * i : 6 + 2 * i] for i in range(4)]
    loads = [
        pltpu.make_async_copy(src, dst, in_sem.at[i])
        for i, (src, dst) in enumerate(
            zip(hbm_in, (kb_ref, kc_ref, bp_ref, fr_ref, q_ref, k_ref, v_ref, do_ref))
        )
    ]
    for i in (2, 3, 5, 6, 4, 7, 0, 1):
        loads[i].start()
    g = lax.axis_index("grp")
    s_id = lax.axis_index("seq")
    z = s_id // 2
    c = s_id % 2
    other = 1 - c
    blk = (c, other)
    steps = (1, -1)

    def at_z(off):
        return lax.rem(z + off + 2 * n_z, n_z)

    def dev(dg=0, dz=0, flip=False):
        core = other if flip else c
        return {"grp": lax.rem(g + dg + n_grp, n_grp), "seq": at_z(dz) * 2 + core}

    sends = []

    def copy(src, dst, sem, at, to):
        return pltpu.make_async_remote_copy(
            src_ref=src,
            dst_ref=dst,
            send_sem=sem[0].at[at],
            recv_sem=sem[1].at[at],
            device_id=to,
            device_id_type=MESH,
        )

    def start(d):
        d.start()
        sends.append(d)

    places = {}

    def ring_copy(src, dst, kind, u, w, key, to):
        at = places.setdefault((kind, u, w), {})
        n = at.setdefault(key, len(at))
        return pltpu.make_async_remote_copy(
            src_ref=src,
            dst_ref=dst,
            send_sem=ring_sem.at[kind, u, w],
            recv_sem=(ag_sem, rs_sem)[kind].at[u, w, n],
            device_id=to,
            device_id_type=MESH,
        )

    barrier = pltpu.get_barrier_semaphore()
    peers = [dev(flip=True), dev(dz=1), dev(dz=-1), dev(dg=1), dev(dg=-1)]
    for p in peers:
        pl.semaphore_signal(barrier, inc=1, device_id=p, device_id_type=MESH)

    def cols(base, width=D):
        return pl.ds(pl.multiple_of(base, D), width)

    def tables(b):
        pos = bp_ref[rows[b]] * BLK + lax.broadcasted_iota(jnp.int32, (BLK, D), 0)
        angle = pos.astype(F32) * fr_ref[...]
        cos_ref[b] = jnp.cos(angle)
        lane = lax.broadcasted_iota(jnp.int32, (BLK, D), 1)
        sin_ref[b] = jnp.where(lane < D // 2, -1.0, 1.0) * jnp.sin(angle)

    row0 = g * GB + 2 * z
    first = (g - 1) * GB
    rows = (row0 + other, row0 + c)
    loads[2].wait()
    loads[3].wait()
    tables(1)
    cos_own, sin_own = cos_ref[1], sin_ref[1]
    loads[5].wait()
    loads[6].wait()

    def rot(x, cs, sn):
        return x * cs + pltpu.roll(x, D // 2, 1) * sn

    def slot(grp, zc, pb):
        return grp * GB + 2 * zc + blk[pb]

    for u in range(2):
        for w in range(2):
            for pb in range(2):
                at = cols((blk[pb] * 2 + u) * D)
                if w == 0:
                    x = rot(k_ref[:, at].astype(F32), cos_own, sin_own).astype(BF)
                else:
                    x = v_ref[:, at]
                if pb == 0:
                    kvs[u][w][slot(1, z, 0)] = x
                else:
                    ks[u, w] = x
    pl.semaphore_wait(barrier, len(peers))

    def kv_chip(u, w, pb):
        return copy(ks.at[u, w], kvs[u][w].at[slot(1, z, pb)], kv_sem, (u, w), dev(flip=True))

    def x_copy(u, which):
        src = q_send.at[:, u * QW : (u + 1) * QW]
        if which == 0:
            src = do_ref.at[:, cols(other * HALF + u * QW, QW)]
        dst = (do_par, q_par)[which].at[:, u * QW : (u + 1) * QW]
        return copy(src, dst, x_sem, (which, u), dev(flip=True))

    def ag_copy(u, w, pb, grp, dr, d, arrived):
        p = kvs[u][w].at[slot(grp, at_z(-steps[dr] * (d if arrived else d - 1)), pb)]
        return ring_copy(p, p, 0, u, w, (pb, grp, dr, d), dev(dz=steps[dr]))

    def ay_copy(u, w, pb, k):
        src = kvs[u][w].at[slot(1, at_z(k), pb)]
        dst = kvs[u][w].at[slot(0, at_z(k), pb)]
        return ring_copy(src, dst, 0, u, w, (pb, k), dev(dg=1))

    def ev_begin(u, w, pb):
        if pb == 1:
            kv_chip(u, w, 1).wait_recv()
        ay_copy(u, w, pb, 0).start()
        for dr in range(2):
            ag_copy(u, w, pb, 1, dr, 1, False).start()

    def ev_own(u, w, pb, dr, k):
        ag_copy(u, w, pb, 1, dr, k, True).wait_recv()
        if k < far_of(dr, pb):
            ag_copy(u, w, pb, 1, dr, k + 1, False).start()
        if k <= reach:
            ay_copy(u, w, pb, -steps[dr] * k).start()

    def ev_prev0(u, w, pb):
        ay_copy(u, w, pb, 0).wait_recv()
        if reach < 1:
            for dr in range(2):
                ag_copy(u, w, pb, 0, dr, 1, False).start()

    def ev_prev(u, w, pb, dr, k):
        if k <= reach:
            ay_copy(u, w, pb, -steps[dr] * k).wait_recv()
        else:
            ag_copy(u, w, pb, 0, dr, k, True).wait_recv()
        if reach < k + 1 <= far_of(dr, pb):
            ag_copy(u, w, pb, 0, dr, k + 1, False).start()

    def q_rope(u):
        if u == 0:
            loads[4].wait()
        for mine in (False, True):
            base = (c if mine else other) * HALF + u * QW
            dst = q_own if mine else q_send
            for h in range(8):
                x = q_ref[:, cols(base + h * D)].astype(F32)
                x = rot(x, cos_own, sin_own) * (SCALE * LOG2E)
                dst[:, u * QW + h * D : u * QW + (h + 1) * D] = x.astype(BF)
            if not mine:
                start(x_copy(u, 1))

    def invert(kb, carry):
        for b in range(2):
            found = jnp.int32(KB)
            for j in range(KB):
                hit = (kb_ref[j, rows[b]] - first == kb) & (j < kc_ref[rows[b]])
                found = jnp.where(hit, j, found)
            inv[b, kb] = found
        return carry

    def setup():
        loads[0].wait()
        loads[1].wait()
        tables(0)
        for b in range(2):
            vg[b, :, D:] = jnp.ones((NK, D), BF)
            for u in range(2):
                for w in range(2):
                    pts[u][w][b, KB] = jnp.zeros((D, BLK), BF)
        lax.fori_loop(0, 2 * GB, invert, 0)

    rr = lax.broadcasted_iota(jnp.int32, (ROWS, BLK), 0) & (BLK - 1)
    cc = lax.broadcasted_iota(jnp.int32, (ROWS, BLK), 1)

    def listed(b, j):
        return jnp.clip(kb_ref[j, rows[b]] - first, 0, 2 * GB - 1)

    def head_rows(half):
        return slice(half * ROWS, (half + 1) * ROWS), [half * 4 + x for x in range(4)]

    def scores(u, b, half):
        if half == 0:
            if b == 0:
                x_copy(u, 1).wait_recv()
            for j in range(KB):
                kg[b, j * BLK : (j + 1) * BLK, :] = kvs[u][0][listed(b, j)]
        count = kc_ref[rows[b]]
        r, heads = head_rows(half)
        src_q = q_par if b == 0 else q_own
        q = jnp.concatenate(
            [src_q[:, u * QW + h * D : u * QW + (h + 1) * D] for h in heads], axis=0
        )
        q_t[b, :, r] = q.T
        mx = None
        for n in range(NK // KW):
            s = nt(q, kg[b, n * KW : (n + 1) * KW, :])
            for t in range(KW // BLK):
                j = n * (KW // BLK) + t
                st = s[:, t * BLK : (t + 1) * BLK]
                if j == 0:
                    st = jnp.where((cc <= rr) & (j < count), st, -1e30)
                else:
                    st = jnp.where(j < count, st, -1e30)
                s_scr[:, j * BLK : (j + 1) * BLK] = st
                mx = st if mx is None else jnp.maximum(mx, st)
        m = jnp.max(mx, axis=1, keepdims=True)
        for j in range(KB):
            ks_ = slice(j * BLK, (j + 1) * BLK)
            e_scr[b, r, ks_] = jnp.exp2(s_scr[:, ks_] - m).astype(BF)

    def attend(u, b, half):
        if half == 0:
            if b == 0:
                x_copy(u, 0).wait_recv()
            for j in range(KB):
                vg[b, j * BLK : (j + 1) * BLK, 0:D] = kvs[u][1][listed(b, j)]
        r, heads = head_rows(half)
        ox = nn(e_scr[b, r, :], vg[b])
        norm = 1.0 / ox[:, D:]
        o = ox[:, :D] * norm
        if b == 0:
            gr = [do_par[:, u * QW + h * D : u * QW + (h + 1) * D] for h in heads]
        else:
            gr = [do_ref[:, cols(c * HALF + u * QW + h * D)] for h in heads]
        gs = (jnp.concatenate(gr, axis=0).astype(F32) * norm).astype(BF)
        do_t[b, :, r] = gs.T
        g_scr[b, r, :] = gs
        delta = jnp.sum(gs.astype(F32) * o, axis=1, keepdims=True)
        dl_scr[b, r, :] = jnp.broadcast_to(delta, (ROWS, D))
        for x, h in enumerate(heads):
            oh = o[x * BLK : (x + 1) * BLK].astype(BF)
            if b == 0:
                o_scr[:, u * QW + h * D : u * QW + (h + 1) * D] = oh
            else:
                out_ref[:, cols(c * HALF + u * QW + h * D)] = oh

    def back(u, b, half):
        r, heads = head_rows(half)
        gs = g_scr[b, r, :]
        delta = dl_scr[b, r, :]
        for n in range(NK // KW):
            dp = nt(gs, vg[b, n * KW : (n + 1) * KW, 0:D])
            for t in range(KW // BLK):
                ks_ = slice(n * KW + t * BLK, n * KW + (t + 1) * BLK)
                x = e_scr[b, r, ks_].astype(F32) * (dp[:, t * BLK : (t + 1) * BLK] - delta)
                ds_scr[b, r, ks_] = x.astype(BF)
        dq = nn(ds_scr[b, r, :], kg[b])
        cs, sn = cos_ref[b] * SCALE, sin_ref[b] * -SCALE
        for x, h in enumerate(heads):
            dh = rot(dq[x * BLK : (x + 1) * BLK], cs, sn).astype(BF)
            if b == 0:
                dq_scr[:, u * QW + h * D : u * QW + (h + 1) * D] = dh
            else:
                qg_ref[:, cols(c * HALF + u * QW + h * D)] = dh

    def o_copy(u, which, core):
        src, dst = ((o_scr, out_ref), (dq_scr, qg_ref))[which]
        return copy(
            src.at[:, u * QW : (u + 1) * QW],
            dst.at[:, cols(core * HALF + u * QW, QW)],
            o_sem,
            (u, which),
            dev(flip=True),
        )

    def grads(w, u, b):
        if b == 0:
            start(o_copy(u, 1 - w, c))
        lhs, rhs = ((q_t, ds_scr), (do_t, e_scr))[w]
        for n in range(NK // KW):
            x = nn(lhs[b], rhs[b, :, n * KW : (n + 1) * KW])
            for t in range(KW // BLK):
                j = n * (KW // BLK) + t
                pts[u][w][b, j] = x[:, t * BLK : (t + 1) * BLK].astype(BF)

    def key_grads(u, b):
        grads(0, u, b)

    def value_grads(u, b):
        grads(1, u, b)

    def do_send(u):
        if u == 0:
            loads[7].wait()
        start(x_copy(u, 0))

    def term(u, w, grp, zc, pb):
        at = slot(grp, zc, pb)
        p = pts[u][w]
        return p[0, inv[0, at]].astype(F32) + p[1, inv[1, at]].astype(F32)

    def rs_copy(u, w, pb, grp, dr, k, arrived=False):
        if k == far_of(dr, pb) and not arrived:
            src = sb.at[u, w, pb, grp, dr]
        else:
            src = rbs[u][w].at[pb, grp, dr, min(k, FAR - 1)]
        dst = rbs[u][w].at[pb, grp, dr, k - 1]
        return ring_copy(src, dst, 1, u, w, (pb, grp, dr, k), dev(dz=steps[dr]))

    def ry_copy(u, w, pb, dr, k):
        at = k if dr == 0 else -k
        src = rbs[u][w].at[pb, 0, dr, k]
        return ring_copy(src, yb.at[u, w, pb, at + 2], 1, u, w, (pb, at), dev(dg=-1))

    def ev_sum_own(u, w, pb, dr, k):
        x = term(u, w, 1, at_z(steps[dr] * k), pb)
        dst = sb.at[u, w, pb, 1, dr]
        if k < far_of(dr, pb):
            rs_copy(u, w, pb, 1, dr, k + 1, True).wait_recv()
            dst = rbs[u][w].at[pb, 1, dr, k]
            x = x + dst[...].astype(F32)
        if k <= reach_r:
            ry_copy(u, w, pb, dr, k).wait_recv()
            x = x + yb[u, w, pb, (k if dr == 0 else -k) + 2].astype(F32)
        dst[...] = x.astype(BF)
        rs_copy(u, w, pb, 1, dr, k).start()

    def ev_sum_prev(u, w, pb, dr, k):
        x = term(u, w, 0, at_z(steps[dr] * k), pb)
        dst = rbs[u][w].at[pb, 0, dr, min(k, FAR - 1)]
        if k >= reach_r and k < far_of(dr, pb):
            rs_copy(u, w, pb, 0, dr, k + 1, True).wait_recv()
            x = x + dst[...].astype(F32)
        elif k > reach_r:
            dst = sb.at[u, w, pb, 0, dr]
        dst[...] = x.astype(BF)
        if k > reach_r:
            rs_copy(u, w, pb, 0, dr, k).start()
        else:
            ry_copy(u, w, pb, dr, k).start()

    def ev_sum_prev0(u, w, pb):
        x = term(u, w, 0, z, pb)
        if reach_r == 0:
            for dr in range(2):
                rs_copy(u, w, pb, 0, dr, 1, True).wait_recv()
                x = x + rbs[u][w][pb, 0, dr, 0].astype(F32)
        rbs[u][w][pb, 0, 0, 0] = x.astype(BF)
        ry_copy(u, w, pb, 0, 0).start()

    def f_copy(u, w):
        return copy(f_s.at[u, w], f_r.at[u, w], f_sem, (u, w), dev(flip=True))

    def ev_sum_home(u, w, pb):
        x = term(u, w, 1, z, pb)
        for dr in range(2):
            rs_copy(u, w, pb, 1, dr, 1, True).wait_recv()
            x = x + rbs[u][w][pb, 1, dr, 0].astype(F32)
        ry_copy(u, w, pb, 0, 0).wait_recv()
        x = x + yb[u, w, pb, 2].astype(F32)
        if pb == 0:
            finish(u, w, c, x)
        else:
            f_s[u, w] = x
            start(f_copy(u, w))

    def ev_finish(u, w, pb):
        if pb == 1:
            f_copy(u, w).wait_recv()
            finish(u, w, other, f_r[u, w])

    def finish(u, w, core, x):
        at = cols((core * 2 + u) * D)
        x = x.T
        if w == 0:
            x = rot(x * (1.0 / LOG2E), cos_own, -sin_own)
            kgr_ref[:, at] = x.astype(BF)
        else:
            vgr_ref[:, at] = x.astype(BF)

    for u in range(2):
        for w in range(2):
            start(kv_chip(u, w, 0))
    events = (
        (ev_begin, 3),
        (ev_own, 5),
        (ev_prev, 5),
        (ev_prev0, 3),
        (ev_sum_own, 5),
        (ev_sum_prev, 5),
        (ev_sum_prev0, 3),
        (ev_sum_home, 3),
        (ev_finish, 3),
        (scores, 3),
        (attend, 3),
        (back, 3),
        (key_grads, 2),
        (value_grads, 2),
        (q_rope, 1),
        (do_send, 1),
        (setup, 0),
    )
    for item in ORDER:
        run, count = events[item // 100000]
        run(*[item // 10 ** (4 - i) % 10 for i in range(count)])
    for u in range(2):
        for which in range(2):
            o_copy(u, which, other).wait_recv()
    for d in sends:
        d.wait_send()
    for kind in range(2):
        for u in range(2):
            for w in range(2):
                assert len(places[kind, u, w]) == PIECES
                every = kvs[u][w].at[pl.ds(0, PIECES)]
                pltpu.make_async_remote_copy(
                    src_ref=every,
                    dst_ref=every,
                    send_sem=ring_sem.at[kind, u, w],
                    recv_sem=ag_sem.at[0, 0, 0],
                    device_id=dev(dz=1),
                    device_id_type=MESH,
                ).wait_send()


def scratch_groups(tok, n_blocks):
    V = pltpu.VMEM
    dma = pltpu.SemaphoreType.DMA
    sems = [dma((8,)), dma((2, 2, 2)), dma((2, 2, PIECES)), dma((2, 2, PIECES))]
    sems += [dma((2, 2))] * 8
    return [
        [V((2 * GB, BLK, D), BF)] * 4,
        [V((2, KB + 1, D, BLK), BF)] * 4,
        [V((2, 2, 2, FAR, D, BLK), BF)] * 4,
        [V((2, 2, BLK, D), BF)] + [V((tok, HALF), BF)] * 6,
        [
            V((2, 2, 2, 2, 2, D, BLK), BF),
            V((2, 2, 2, 5, D, BLK), BF),
            V((2, 2, D, BLK), F32),
            V((2, 2, D, BLK), F32),
        ],
        [
            pltpu.SMEM((KB, n_blocks), jnp.int32),
            pltpu.SMEM((n_blocks,), jnp.int32),
            pltpu.SMEM((n_blocks,), jnp.int32),
            V((1, D), F32),
            V((tok, HEADS * D), BF),
            V((tok, KV_HEADS * D), BF),
            V((tok, KV_HEADS * D), BF),
            V((tok, HEADS * D), BF),
            V((2, BLK, D), F32),
            V((2, BLK, D), F32),
        ],
        [
            V((2, NK, D), BF),
            V((2, NK, 2 * D), BF),
            V((ROWS, NK), F32),
            V((2, 8 * BLK, NK), BF),
            V((2, 8 * BLK, NK), BF),
            V((2, D, 8 * BLK), BF),
            V((2, D, 8 * BLK), BF),
            V((2, 8 * BLK, D), BF),
            V((2, 8 * BLK, D), F32),
            pltpu.SMEM((2, 2 * GB), jnp.int32),
        ],
        sems,
    ]


def split(refs):
    out, at = [], 0
    for n in [8, 4] + [len(x) for x in scratch_groups(BLK, 2 * GB)]:
        out.append(refs[at : at + n])
        at += n
    return out


def store(*refs):
    copies = [pltpu.make_async_copy(refs[i], refs[4 + i], refs[8].at[i]) for i in range(4)]
    for d in copies:
        d.start()
    for d in copies:
        d.wait()


def local(n_grp, n_seq, q, k, v, do, key_blocks, key_counts, block_position):
    vm = pl.BlockSpec(memory_space=pltpu.VMEM)
    hbm = pl.BlockSpec(memory_space=pltpu.HBM)
    scratch = [x for group in scratch_groups(q.shape[0], key_counts.shape[0]) for x in group]
    shapes = [jax.ShapeDtypeStruct(x.shape, BF) for x in (q, q, k, k)]
    operands = [
        pltpu.with_memory_space_constraint(x, pltpu.HBM)
        for x in (key_blocks.T, key_counts, block_position, jnp.asarray(FREQ), q, k, v, do)
    ]
    results = pl.pallas_call(
        functools.partial(kernel, n_grp, n_seq // 2, REACH, REACH_R),
        out_shape=shapes,
        in_specs=[hbm] * 8,
        out_specs=[vm] * 4,
        scratch_shapes=scratch,
        compiler_params=pltpu.CompilerParams(
            collective_id=0, has_side_effects=True, vmem_limit_bytes=48 * 2**20
        ),
    )(*operands)
    return pl.pallas_call(
        store,
        out_shape=shapes,
        in_specs=[pl.BlockSpec(memory_space=pl.ANY)] * 4,
        out_specs=[hbm] * 4,
        scratch_shapes=[pltpu.SemaphoreType.DMA((4,))],
        compiler_params=pltpu.CompilerParams(vmem_limit_bytes=2**20),
    )(*results)


def solution(mesh):
    rows = P(("grp", "seq"), None)
    return jax.shard_map(
        functools.partial(local, mesh.shape["grp"], mesh.shape["seq"]),
        mesh=mesh,
        in_specs=(rows, rows, rows, rows, P(), P(), P()),
        out_specs=(rows, rows, rows, rows),
        check_vma=False,
    )
```

```python
import functools
import math

import jax
import jax.numpy as jnp
import numpy as np
from jax import lax
from jax.experimental import pallas as pl
from jax.experimental.pallas import tpu as pltpu
from jax.sharding import PartitionSpec as P

HEADS = 32
KV_HEADS = 4
D = 128
BLK = 128
KB = 12
GB = 16
NK = KB * BLK
HALF = HEADS * D // 2
QW = 8 * D
KW = 256
ROWS = 512
MESH = pl.DeviceIdType.MESH
BF = jnp.bfloat16
F32 = jnp.float32
LOG2E = 1.0 / math.log(2.0)
SCALE = 1.0 / math.sqrt(D)
PIECES = 30
FREQ = np.tile(500000.0 ** (-np.arange(D // 2) / (D // 2)), 2).astype(np.float32)[None]
FAR = 4
REACH = (2, 3)
REACH_R = (2, 2)
MAX_REACH = 3
ORDER = (
    0, 1000, 100, 1100, 1600000, 1500000, 100001, 100011, 1400000, 101001, 300000, 100111, 101111,
    101011, 100101, 100012, 100002, 1410000, 100112, 101002, 101112, 101101, 101012, 100102,
    10100, 10000, 1700000, 100013, 200012, 100003, 300100, 101113, 200002, 200101, 101102,
    1800000, 101003, 301100, 200112, 100103, 100113, 110001, 201001, 201002, 110011, 201112,
    200003, 201012, 100004, 200113, 101103, 1510000, 200102, 110111, 200001, 11100, 11000, 201003,
    110012, 200111, 201101, 110002, 101114, 310100, 201102, 200013, 201111, 100114, 201013,
    200011, 200004, 201011, 301000, 310000, 101013, 110101, 201113, 210001, 101004, 200114,
    200103, 901000, 900000, 110112, 111001, 900100, 111111, 111011, 901100, 311100, 201004,
    201114, 110003, 201103, 1000000, 1001000, 110113, 110102, 1000100, 111002, 1001100, 111112,
    111101, 210012, 1300000, 110013, 1301000, 501114, 401004, 501013, 501004, 1101000, 601100,
    211011, 401114, 110103, 210003, 501103, 111003, 1100000, 210113, 111102, 1101100, 501113,
    501003, 111113, 111012, 210011, 501101, 601000, 1100100, 110004, 210111, 401003, 501012,
    501102, 211001, 401013, 1200000, 401103, 110114, 210112, 1201000, 800000, 311000, 210114,
    210013, 210004, 401113, 210002, 500004, 500011, 210103, 211101, 210102, 210101, 211111,
    211002, 111004, 501112, 500001, 501011, 500013, 500111, 400004, 600000, 111103, 910000,
    211003, 500103, 501002, 500101, 111013, 211102, 501111, 600100, 211113, 911000, 401102,
    501001, 911100, 400114, 400103, 801000, 401012, 211103, 910100, 500114, 211112, 111114,
    401112, 211013, 500003, 211012, 211114, 211004, 1011000, 400013, 500012, 1010000, 1011100,
    401101, 1010100, 400113, 500102, 1310000, 500002, 500113, 1311000, 511114, 411004, 411114,
    511013, 511004, 511001, 401002, 411103, 511103, 511111, 1110000, 401111, 1111000, 511101,
    411013, 401011, 611000, 611100, 400003, 400012, 400102, 1111100, 511113, 500112, 511011,
    411003, 411113, 1211000, 1110100, 1210000, 510114, 510004, 511012, 511003, 511102, 510013,
    510103, 410004, 400002, 410114, 511112, 610000, 510101, 400112, 510113, 510003, 510012,
    411012, 401001, 511002, 510102, 410113, 410103, 411102, 400011, 510112, 410013, 410003,
    400101, 510002, 811000, 701100, 400001, 411112, 810000, 610100, 410102, 400111, 411002,
    510111, 410112, 410012, 411011, 510011, 801100, 510001, 411111, 410002, 411101, 410101,
    700100, 410111, 411001, 700000, 410011, 410001, 711100, 800100, 710100, 701000, 711000,
    811100, 710000, 810100,
)


def nt(a, b):
    return lax.dot_general(a, b, (((1,), (1,)), ((), ())), preferred_element_type=F32)


def nn(a, b):
    return lax.dot_general(a, b, (((1,), (0,)), ((), ())), preferred_element_type=F32)


def far_of(dr, pb):
    return FAR if dr == pb else FAR - 1


def kernel(n_grp, n_z, reach, reach_r, *refs):
    (
        hbm_in,
        (out_ref, qg_ref, kgr_ref, vgr_ref),
        kvs,
        pts,
        rbs,
        (ks, q_own, q_send, q_par, do_par, o_scr, dq_scr),
        (sb, yb, f_s, f_r),
        (kb_ref, kc_ref, bp_ref, fr_ref, q_ref, k_ref, v_ref, do_ref, cos_ref, sin_ref),
        (kg, vg, s_scr, e_scr, ds_scr, q_t, do_t, g_scr, dl_scr, inv),
        sems,
    ) = split(refs)
    kvs = (kvs[0:2], kvs[2:4])
    pts = (pts[0:2], pts[2:4])
    rbs = (rbs[0:2], rbs[2:4])
    in_sem, ring_sem, ag_sem, rs_sem = sems[:4]
    kv_sem, x_sem, f_sem, o_sem = [sems[4 + 2 * i : 6 + 2 * i] for i in range(4)]
    loads = [
        pltpu.make_async_copy(src, dst, in_sem.at[i])
        for i, (src, dst) in enumerate(
            zip(hbm_in, (kb_ref, kc_ref, bp_ref, fr_ref, q_ref, k_ref, v_ref, do_ref))
        )
    ]
    for i in (2, 3, 5, 6, 4, 7, 0, 1):
        loads[i].start()
    g = lax.axis_index("grp")
    s_id = lax.axis_index("seq")
    z = s_id // 2
    c = s_id % 2
    other = 1 - c
    blk = (c, other)
    steps = (1, -1)

    def at_z(off):
        return lax.rem(z + off + 2 * n_z, n_z)

    def dev(dg=0, dz=0, flip=False):
        core = other if flip else c
        return {"grp": lax.rem(g + dg + n_grp, n_grp), "seq": at_z(dz) * 2 + core}

    sends = []

    def copy(src, dst, sem, at, to):
        return pltpu.make_async_remote_copy(
            src_ref=src,
            dst_ref=dst,
            send_sem=sem[0].at[at],
            recv_sem=sem[1].at[at],
            device_id=to,
            device_id_type=MESH,
        )

    def start(d):
        d.start()
        sends.append(d)

    places = {}

    def ring_copy(src, dst, kind, u, w, key, to):
        at = places.setdefault((kind, u, w), {})
        n = at.setdefault(key, len(at))
        return pltpu.make_async_remote_copy(
            src_ref=src,
            dst_ref=dst,
            send_sem=ring_sem.at[kind, u, w],
            recv_sem=(ag_sem, rs_sem)[kind].at[u, w, n],
            device_id=to,
            device_id_type=MESH,
        )

    barrier = pltpu.get_barrier_semaphore()
    peers = [dev(flip=True), dev(dz=1), dev(dz=-1), dev(dg=1), dev(dg=-1)]
    for p in peers:
        pl.semaphore_signal(barrier, inc=1, device_id=p, device_id_type=MESH)

    def cols(base, width=D):
        return pl.ds(pl.multiple_of(base, D), width)

    def tables(b):
        pos = bp_ref[rows[b]] * BLK + lax.broadcasted_iota(jnp.int32, (BLK, D), 0)
        angle = pos.astype(F32) * fr_ref[...]
        cos_ref[b] = jnp.cos(angle)
        lane = lax.broadcasted_iota(jnp.int32, (BLK, D), 1)
        sin_ref[b] = jnp.where(lane < D // 2, -1.0, 1.0) * jnp.sin(angle)

    row0 = g * GB + 2 * z
    first = (g - 1) * GB
    rows = (row0 + other, row0 + c)
    loads[2].wait()
    loads[3].wait()
    tables(1)
    cos_own, sin_own = cos_ref[1], sin_ref[1]
    loads[5].wait()
    loads[6].wait()

    def rot(x, cs, sn):
        return x * cs + pltpu.roll(x, D // 2, 1) * sn

    def slot(grp, zc, pb):
        return grp * GB + 2 * zc + blk[pb]

    for u in range(2):
        for w in range(2):
            for pb in range(2):
                at = cols((blk[pb] * 2 + u) * D)
                if w == 0:
                    x = rot(k_ref[:, at].astype(F32), cos_own, sin_own).astype(BF)
                else:
                    x = v_ref[:, at]
                if pb == 0:
                    kvs[u][w][slot(1, z, 0)] = x
                else:
                    ks[u, w] = x
    loads[0].wait()
    loads[1].wait()
    pl.semaphore_wait(barrier, len(peers))

    def kv_chip(u, w, pb):
        return copy(ks.at[u, w], kvs[u][w].at[slot(1, z, pb)], kv_sem, (u, w), dev(flip=True))

    def x_copy(u, which):
        src = q_send.at[:, u * QW : (u + 1) * QW]
        if which == 0:
            src = do_ref.at[:, cols(other * HALF + u * QW, QW)]
        dst = (do_par, q_par)[which].at[:, u * QW : (u + 1) * QW]
        return copy(src, dst, x_sem, (which, u), dev(flip=True))

    def ag_copy(u, w, pb, grp, dr, d, arrived):
        p = kvs[u][w].at[slot(grp, at_z(-steps[dr] * (d if arrived else d - 1)), pb)]
        return ring_copy(p, p, 0, u, w, (pb, grp, dr, d), dev(dz=steps[dr]))

    def ay_copy(u, w, pb, k):
        src = kvs[u][w].at[slot(1, at_z(k), pb)]
        dst = kvs[u][w].at[slot(0, at_z(k), pb)]
        return ring_copy(src, dst, 0, u, w, (pb, k), dev(dg=1))

    def ev_begin(u, w, pb):
        if pb == 1:
            kv_chip(u, w, 1).wait_recv()
        ay_copy(u, w, pb, 0).start()
        for dr in range(2):
            ag_copy(u, w, pb, 1, dr, 1, False).start()

    def ev_own(u, w, pb, dr, k):
        ag_copy(u, w, pb, 1, dr, k, True).wait_recv()
        if k < far_of(dr, pb):
            ag_copy(u, w, pb, 1, dr, k + 1, False).start()
        if k <= reach[u]:
            ay_copy(u, w, pb, -steps[dr] * k).start()

    def ev_prev0(u, w, pb):
        ay_copy(u, w, pb, 0).wait_recv()
        if reach[u] < 1:
            for dr in range(2):
                ag_copy(u, w, pb, 0, dr, 1, False).start()

    def ev_prev(u, w, pb, dr, k):
        if k <= reach[u]:
            ay_copy(u, w, pb, -steps[dr] * k).wait_recv()
        else:
            ag_copy(u, w, pb, 0, dr, k, True).wait_recv()
        if reach[u] < k + 1 <= far_of(dr, pb):
            ag_copy(u, w, pb, 0, dr, k + 1, False).start()

    def q_rope(u):
        if u == 0:
            loads[4].wait()
        for mine in (False, True):
            base = (c if mine else other) * HALF + u * QW
            dst = q_own if mine else q_send
            for h in range(8):
                x = q_ref[:, cols(base + h * D)].astype(F32)
                x = rot(x, cos_own, sin_own) * (SCALE * LOG2E)
                dst[:, u * QW + h * D : u * QW + (h + 1) * D] = x.astype(BF)
            if not mine:
                start(x_copy(u, 1))

    def invert(kb, carry):
        for b in range(2):
            found = jnp.int32(KB)
            for j in range(KB):
                hit = (kb_ref[j, rows[b]] - first == kb) & (j < kc_ref[rows[b]])
                found = jnp.where(hit, j, found)
            inv[b, kb] = found
        return carry

    def invert_all():
        for b in range(2):
            for u in range(2):
                for w in range(2):
                    pts[u][w][b, KB] = jnp.zeros((D, BLK), BF)
        lax.fori_loop(0, 2 * GB, invert, 0)

    def set_ones():
        for b in range(2):
            vg[b, :, D:] = jnp.ones((NK, D), BF)

    rr = lax.broadcasted_iota(jnp.int32, (ROWS, BLK), 0) & (BLK - 1)
    cc = lax.broadcasted_iota(jnp.int32, (ROWS, BLK), 1)

    def listed(b, j):
        return jnp.clip(kb_ref[j, rows[b]] - first, 0, 2 * GB - 1)

    def head_rows(half):
        return slice(half * ROWS, (half + 1) * ROWS), [half * 4 + x for x in range(4)]

    def scores(u, b, half):
        if half == 0:
            if b == 0:
                x_copy(u, 1).wait_recv()
            for j in range(KB):
                kg[b, j * BLK : (j + 1) * BLK, :] = kvs[u][0][listed(b, j)]
        count = kc_ref[rows[b]]
        r, heads = head_rows(half)
        src_q = q_par if b == 0 else q_own
        q = jnp.concatenate(
            [src_q[:, u * QW + h * D : u * QW + (h + 1) * D] for h in heads], axis=0
        )
        q_t[b, :, r] = q.T
        mx = None
        for n in range(NK // KW):
            s = nt(q, kg[b, n * KW : (n + 1) * KW, :])
            for t in range(KW // BLK):
                j = n * (KW // BLK) + t
                st = s[:, t * BLK : (t + 1) * BLK]
                if j == 0:
                    st = jnp.where((cc <= rr) & (j < count), st, -1e30)
                else:
                    st = jnp.where(j < count, st, -1e30)
                s_scr[:, j * BLK : (j + 1) * BLK] = st
                mx = st if mx is None else jnp.maximum(mx, st)
        m = jnp.max(mx, axis=1, keepdims=True)
        for j in range(KB):
            ks_ = slice(j * BLK, (j + 1) * BLK)
            e_scr[b, r, ks_] = jnp.exp2(s_scr[:, ks_] - m).astype(BF)

    def attend(u, b, half):
        if half == 0:
            if b == 0:
                x_copy(u, 0).wait_recv()
            for j in range(KB):
                vg[b, j * BLK : (j + 1) * BLK, 0:D] = kvs[u][1][listed(b, j)]
        r, heads = head_rows(half)
        ox = nn(e_scr[b, r, :], vg[b])
        norm = 1.0 / ox[:, D:]
        o = ox[:, :D] * norm
        if b == 0:
            gr = [do_par[:, u * QW + h * D : u * QW + (h + 1) * D] for h in heads]
        else:
            gr = [do_ref[:, cols(c * HALF + u * QW + h * D)] for h in heads]
        gs = (jnp.concatenate(gr, axis=0).astype(F32) * norm).astype(BF)
        do_t[b, :, r] = gs.T
        g_scr[b, r, :] = gs
        delta = jnp.sum(gs.astype(F32) * o, axis=1, keepdims=True)
        dl_scr[b, r, :] = jnp.broadcast_to(delta, (ROWS, D))
        for x, h in enumerate(heads):
            oh = o[x * BLK : (x + 1) * BLK].astype(BF)
            if b == 0:
                o_scr[:, u * QW + h * D : u * QW + (h + 1) * D] = oh
            else:
                out_ref[:, cols(c * HALF + u * QW + h * D)] = oh

    def back(u, b, half):
        r, heads = head_rows(half)
        gs = g_scr[b, r, :]
        delta = dl_scr[b, r, :]
        for n in range(NK // KW):
            dp = nt(gs, vg[b, n * KW : (n + 1) * KW, 0:D])
            for t in range(KW // BLK):
                ks_ = slice(n * KW + t * BLK, n * KW + (t + 1) * BLK)
                x = e_scr[b, r, ks_].astype(F32) * (dp[:, t * BLK : (t + 1) * BLK] - delta)
                ds_scr[b, r, ks_] = x.astype(BF)
        dq = nn(ds_scr[b, r, :], kg[b])
        cs, sn = cos_ref[b] * SCALE, sin_ref[b] * -SCALE
        for x, h in enumerate(heads):
            dh = rot(dq[x * BLK : (x + 1) * BLK], cs, sn).astype(BF)
            if b == 0:
                dq_scr[:, u * QW + h * D : u * QW + (h + 1) * D] = dh
            else:
                qg_ref[:, cols(c * HALF + u * QW + h * D)] = dh

    def o_copy(u, which, core):
        src, dst = ((o_scr, out_ref), (dq_scr, qg_ref))[which]
        return copy(
            src.at[:, u * QW : (u + 1) * QW],
            dst.at[:, cols(core * HALF + u * QW, QW)],
            o_sem,
            (u, which),
            dev(flip=True),
        )

    def grads(w, u, b):
        if b == 0:
            start(o_copy(u, 1 - w, c))
        lhs, rhs = ((q_t, ds_scr), (do_t, e_scr))[w]
        for n in range(NK // KW):
            x = nn(lhs[b], rhs[b, :, n * KW : (n + 1) * KW])
            for t in range(KW // BLK):
                j = n * (KW // BLK) + t
                pts[u][w][b, j] = x[:, t * BLK : (t + 1) * BLK].astype(BF)

    def key_grads(u, b):
        grads(0, u, b)

    def value_grads(u, b):
        grads(1, u, b)

    def do_send(u):
        if u == 0:
            loads[7].wait()
        start(x_copy(u, 0))

    def term(u, w, grp, zc, pb):
        at = slot(grp, zc, pb)
        p = pts[u][w]
        return p[0, inv[0, at]].astype(F32) + p[1, inv[1, at]].astype(F32)

    def rs_copy(u, w, pb, grp, dr, k, arrived=False):
        if k == far_of(dr, pb) and not arrived:
            src = sb.at[u, w, pb, grp, dr]
        else:
            src = rbs[u][w].at[pb, grp, dr, min(k, FAR - 1)]
        dst = rbs[u][w].at[pb, grp, dr, k - 1]
        return ring_copy(src, dst, 1, u, w, (pb, grp, dr, k), dev(dz=steps[dr]))

    def ry_copy(u, w, pb, dr, k):
        at = k if dr == 0 else -k
        src = rbs[u][w].at[pb, 0, dr, k]
        return ring_copy(src, yb.at[u, w, pb, at + MAX_REACH], 1, u, w, (pb, at), dev(dg=-1))

    def ev_sum_own(u, w, pb, dr, k):
        x = term(u, w, 1, at_z(steps[dr] * k), pb)
        dst = sb.at[u, w, pb, 1, dr]
        if k < far_of(dr, pb):
            rs_copy(u, w, pb, 1, dr, k + 1, True).wait_recv()
            dst = rbs[u][w].at[pb, 1, dr, k]
            x = x + dst[...].astype(F32)
        if k <= reach_r[u]:
            ry_copy(u, w, pb, dr, k).wait_recv()
            x = x + yb[u, w, pb, (k if dr == 0 else -k) + MAX_REACH].astype(F32)
        dst[...] = x.astype(BF)
        rs_copy(u, w, pb, 1, dr, k).start()

    def ev_sum_prev(u, w, pb, dr, k):
        x = term(u, w, 0, at_z(steps[dr] * k), pb)
        dst = rbs[u][w].at[pb, 0, dr, min(k, FAR - 1)]
        if k >= reach_r[u] and k < far_of(dr, pb):
            rs_copy(u, w, pb, 0, dr, k + 1, True).wait_recv()
            x = x + dst[...].astype(F32)
        elif k > reach_r[u]:
            dst = sb.at[u, w, pb, 0, dr]
        dst[...] = x.astype(BF)
        if k > reach_r[u]:
            rs_copy(u, w, pb, 0, dr, k).start()
        else:
            ry_copy(u, w, pb, dr, k).start()

    def ev_sum_prev0(u, w, pb):
        x = term(u, w, 0, z, pb)
        if reach_r[u] == 0:
            for dr in range(2):
                rs_copy(u, w, pb, 0, dr, 1, True).wait_recv()
                x = x + rbs[u][w][pb, 0, dr, 0].astype(F32)
        rbs[u][w][pb, 0, 0, 0] = x.astype(BF)
        ry_copy(u, w, pb, 0, 0).start()

    def f_copy(u, w):
        return copy(f_s.at[u, w], f_r.at[u, w], f_sem, (u, w), dev(flip=True))

    def ev_sum_home(u, w, pb):
        x = term(u, w, 1, z, pb)
        for dr in range(2):
            rs_copy(u, w, pb, 1, dr, 1, True).wait_recv()
            x = x + rbs[u][w][pb, 1, dr, 0].astype(F32)
        ry_copy(u, w, pb, 0, 0).wait_recv()
        x = x + yb[u, w, pb, MAX_REACH].astype(F32)
        if pb == 0:
            finish(u, w, c, x)
        else:
            f_s[u, w] = x
            start(f_copy(u, w))

    def ev_finish(u, w, pb):
        if pb == 1:
            f_copy(u, w).wait_recv()
            finish(u, w, other, f_r[u, w])

    def finish(u, w, core, x):
        at = cols((core * 2 + u) * D)
        x = x.T
        if w == 0:
            x = rot(x * (1.0 / LOG2E), cos_own, -sin_own)
            kgr_ref[:, at] = x.astype(BF)
        else:
            vgr_ref[:, at] = x.astype(BF)

    for u in range(2):
        for w in range(2):
            start(kv_chip(u, w, 0))
    events = (
        (ev_begin, 3),
        (ev_own, 5),
        (ev_prev, 5),
        (ev_prev0, 3),
        (ev_sum_own, 5),
        (ev_sum_prev, 5),
        (ev_sum_prev0, 3),
        (ev_sum_home, 3),
        (ev_finish, 3),
        (scores, 3),
        (attend, 3),
        (back, 3),
        (key_grads, 2),
        (value_grads, 2),
        (q_rope, 1),
        (do_send, 1),
        (functools.partial(tables, 0), 0),
        (invert_all, 0),
        (set_ones, 0),
    )
    for item in ORDER:
        run, count = events[item // 100000]
        run(*[item // 10 ** (4 - i) % 10 for i in range(count)])
    for u in range(2):
        for which in range(2):
            o_copy(u, which, other).wait_recv()
    for d in sends:
        d.wait_send()
    for kind in range(2):
        for u in range(2):
            for w in range(2):
                assert len(places[kind, u, w]) == PIECES
                every = kvs[u][w].at[pl.ds(0, PIECES)]
                pltpu.make_async_remote_copy(
                    src_ref=every,
                    dst_ref=every,
                    send_sem=ring_sem.at[kind, u, w],
                    recv_sem=ag_sem.at[0, 0, 0],
                    device_id=dev(dz=1),
                    device_id_type=MESH,
                ).wait_send()


def scratch_groups(tok, n_blocks):
    V = pltpu.VMEM
    dma = pltpu.SemaphoreType.DMA
    sems = [dma((8,)), dma((2, 2, 2)), dma((2, 2, PIECES)), dma((2, 2, PIECES))]
    sems += [dma((2, 2))] * 8
    return [
        [V((2 * GB, BLK, D), BF)] * 4,
        [V((2, KB + 1, D, BLK), BF)] * 4,
        [V((2, 2, 2, FAR, D, BLK), BF)] * 4,
        [V((2, 2, BLK, D), BF)] + [V((tok, HALF), BF)] * 6,
        [
            V((2, 2, 2, 2, 2, D, BLK), BF),
            V((2, 2, 2, 2 * MAX_REACH + 1, D, BLK), BF),
            V((2, 2, D, BLK), F32),
            V((2, 2, D, BLK), F32),
        ],
        [
            pltpu.SMEM((KB, n_blocks), jnp.int32),
            pltpu.SMEM((n_blocks,), jnp.int32),
            pltpu.SMEM((n_blocks,), jnp.int32),
            V((1, D), F32),
            V((tok, HEADS * D), BF),
            V((tok, KV_HEADS * D), BF),
            V((tok, KV_HEADS * D), BF),
            V((tok, HEADS * D), BF),
            V((2, BLK, D), F32),
            V((2, BLK, D), F32),
        ],
        [
            V((2, NK, D), BF),
            V((2, NK, 2 * D), BF),
            V((ROWS, NK), F32),
            V((2, 8 * BLK, NK), BF),
            V((2, 8 * BLK, NK), BF),
            V((2, D, 8 * BLK), BF),
            V((2, D, 8 * BLK), BF),
            V((2, 8 * BLK, D), BF),
            V((2, 8 * BLK, D), F32),
            pltpu.SMEM((2, 2 * GB), jnp.int32),
        ],
        sems,
    ]


def split(refs):
    out, at = [], 0
    for n in [8, 4] + [len(x) for x in scratch_groups(BLK, 2 * GB)]:
        out.append(refs[at : at + n])
        at += n
    return out


def store(*refs):
    copies = [pltpu.make_async_copy(refs[i], refs[4 + i], refs[8].at[i]) for i in range(4)]
    for d in copies:
        d.start()
    for d in copies:
        d.wait()


def local(n_grp, n_seq, q, k, v, do, key_blocks, key_counts, block_position):
    vm = pl.BlockSpec(memory_space=pltpu.VMEM)
    hbm = pl.BlockSpec(memory_space=pltpu.HBM)
    scratch = [x for group in scratch_groups(q.shape[0], key_counts.shape[0]) for x in group]
    shapes = [jax.ShapeDtypeStruct(x.shape, BF) for x in (q, q, k, k)]
    operands = [
        pltpu.with_memory_space_constraint(x, pltpu.HBM)
        for x in (key_blocks.T, key_counts, block_position, jnp.asarray(FREQ), q, k, v, do)
    ]
    results = pl.pallas_call(
        functools.partial(kernel, n_grp, n_seq // 2, REACH, REACH_R),
        out_shape=shapes,
        in_specs=[hbm] * 8,
        out_specs=[vm] * 4,
        scratch_shapes=scratch,
        compiler_params=pltpu.CompilerParams(
            collective_id=0, has_side_effects=True, vmem_limit_bytes=48 * 2**20
        ),
    )(*operands)
    return pl.pallas_call(
        store,
        out_shape=shapes,
        in_specs=[pl.BlockSpec(memory_space=pl.ANY)] * 4,
        out_specs=[hbm] * 4,
        scratch_shapes=[pltpu.SemaphoreType.DMA((4,))],
        compiler_params=pltpu.CompilerParams(vmem_limit_bytes=2**20),
    )(*results)


def solution(mesh):
    rows = P(("grp", "seq"), None)
    return jax.shard_map(
        functools.partial(local, mesh.shape["grp"], mesh.shape["seq"]),
        mesh=mesh,
        in_specs=(rows, rows, rows, rows, P(), P(), P()),
        out_specs=(rows, rows, rows, rows),
        check_vma=False,
    )
```

```python
import functools
import math

import jax
import jax.numpy as jnp
import numpy as np
from jax import lax
from jax.experimental import pallas as pl
from jax.experimental.pallas import tpu as pltpu
from jax.sharding import PartitionSpec as P

HEADS = 32
KV_HEADS = 4
D = 128
BLK = 128
KB = 12
GB = 16
NK = KB * BLK
HALF = HEADS * D // 2
QW = 8 * D
KW = 256
ROWS = 512
MESH = pl.DeviceIdType.MESH
BF = jnp.bfloat16
F32 = jnp.float32
LOG2E = 1.0 / math.log(2.0)
SCALE = 1.0 / math.sqrt(D)
PIECES = 30
FREQ = np.tile(500000.0 ** (-np.arange(D // 2) / (D // 2)), 2).astype(np.float32)[None]
FAR = 4
REACH = (2, 3)
REACH_R = (2, 2)
MAX_REACH = 3
ORDER = (
    0, 1000, 1400000, 100, 1100, 10100, 1700000, 100001, 101001, 100011, 1800000, 100111, 101111,
    100101, 1600000, 101011, 200001, 100002, 100112, 101002, 100102, 101112, 1500000, 100012,
    101101, 101012, 110111, 100003, 10000, 201011, 101003, 200002, 200112, 100113, 101113, 101102,
    201002, 200011, 1410000, 200102, 110001, 201112, 200012, 200113, 200003, 11000, 201003,
    100103, 310100, 110112, 301000, 201101, 101013, 11100, 101103, 200013, 210111, 201113, 100013,
    201012, 200111, 101114, 301100, 100114, 300100, 201111, 200101, 110002, 200103, 100004,
    300000, 101004, 310000, 201001, 110011, 200004, 201102, 110101, 200114, 900000, 900100,
    111001, 901000, 110113, 111111, 201004, 901100, 201013, 111011, 201103, 201114, 110003,
    1000000, 1000100, 111002, 110102, 210011, 1001000, 1001100, 110012, 111101, 111112, 1300000,
    1301000, 501004, 1101000, 111003, 210003, 501111, 311100, 501114, 501013, 311000, 111012,
    501103, 211111, 210113, 1101100, 111113, 110103, 210001, 210012, 1201000, 401114, 110013,
    210101, 210112, 210002, 501003, 111102, 501011, 110004, 1100000, 110114, 501001, 1510000,
    1100100, 501101, 401004, 501113, 1200000, 210114, 211113, 501102, 501012, 211003, 500103,
    210102, 500011, 500004, 801000, 211011, 210004, 210103, 500001, 211002, 400103, 500013,
    601000, 211112, 210013, 211001, 111103, 401103, 111013, 500111, 400114, 401013, 500114,
    911000, 400004, 910000, 910100, 211012, 401003, 211102, 211114, 911100, 501002, 500102,
    801100, 501112, 400013, 211101, 401113, 211013, 211004, 500012, 211103, 111004, 111114,
    1011000, 1010000, 601100, 600000, 1011100, 500003, 401102, 500101, 1010100, 500113, 1311000,
    401012, 1310000, 511004, 511013, 401002, 511103, 411103, 511114, 1111000, 611100, 400113,
    600100, 411013, 1111100, 411004, 400012, 511101, 411114, 400003, 511011, 1110000, 500112,
    511012, 511113, 401101, 401001, 401011, 401112, 511003, 1110100, 511001, 1211000, 511111,
    400102, 400011, 1210000, 510004, 510114, 511102, 410114, 410004, 510013, 810000, 510103,
    510101, 511002, 610100, 811100, 410013, 500002, 511112, 411003, 510003, 800100, 510113,
    810100, 701000, 410103, 411102, 410003, 411113, 410113, 411012, 510012, 411002, 510102,
    510002, 400112, 510112, 400002, 401111, 510001, 510011, 800000, 510111, 411112, 411101,
    410012, 410102, 411011, 410002, 411001, 400101, 811000, 410112, 400111, 411111, 400001,
    410011, 611000, 410001, 610000, 410101, 410111, 711100, 700100, 701100, 710000, 700000,
    711000, 710100,
)


def nt(a, b):
    return lax.dot_general(a, b, (((1,), (1,)), ((), ())), preferred_element_type=F32)


def nn(a, b):
    return lax.dot_general(a, b, (((1,), (0,)), ((), ())), preferred_element_type=F32)


def far_of(dr, pb):
    return FAR if dr == pb else FAR - 1


def kernel(n_grp, n_z, reach, reach_r, *refs):
    (
        hbm_in,
        (out_ref, qg_ref, kgr_ref, vgr_ref),
        kvs,
        pts,
        rbs,
        (ks, q_own, q_send, q_par, do_par, o_scr, dq_scr),
        (sb, yb, f_s, f_r),
        (kb_ref, kc_ref, bp_ref, fr_ref, q_ref, k_ref, v_ref, do_ref, cos_ref, sin_ref),
        (kg, vg, s_scr, e_scr, ds_scr, q_t, do_t, g_scr, dl_scr, inv),
        sems,
    ) = split(refs)
    kvs = (kvs[0:2], kvs[2:4])
    pts = (pts[0:2], pts[2:4])
    rbs = (rbs[0:2], rbs[2:4])
    in_sem, ring_sem, ag_sem, rs_sem = sems[:4]
    kv_sem, x_sem, f_sem, o_sem = [sems[4 + 2 * i : 6 + 2 * i] for i in range(4)]
    loads = [
        pltpu.make_async_copy(src, dst, in_sem.at[i])
        for i, (src, dst) in enumerate(
            zip(hbm_in, (kb_ref, kc_ref, bp_ref, fr_ref, q_ref, k_ref, v_ref, do_ref))
        )
    ]
    for i in (2, 3, 5, 6, 4, 7, 0, 1):
        loads[i].start()
    g = lax.axis_index("grp")
    s_id = lax.axis_index("seq")
    z = s_id // 2
    c = s_id % 2
    other = 1 - c
    blk = (c, other)
    steps = (1, -1)

    turns, devices = {}, {}

    def at_z(off):
        if off not in turns:
            turns[off] = lax.rem(z + (off + 2 * n_z), n_z)
        return turns[off]

    def dev(dg=0, dz=0, flip=False):
        at = (dg, dz, flip)
        if at not in devices:
            core = other if flip else c
            devices[at] = {"grp": lax.rem(g + (dg + n_grp), n_grp), "seq": at_z(dz) * 2 + core}
        return devices[at]

    sends = []

    def copy(src, dst, sem, at, to):
        return pltpu.make_async_remote_copy(
            src_ref=src,
            dst_ref=dst,
            send_sem=sem[0].at[at],
            recv_sem=sem[1].at[at],
            device_id=to,
            device_id_type=MESH,
        )

    def start(d):
        d.start()
        sends.append(d)

    places = {}

    def ring_copy(src, dst, kind, u, w, key, to):
        at = places.setdefault((kind, u, w), {})
        n = at.setdefault(key, len(at))
        return pltpu.make_async_remote_copy(
            src_ref=src,
            dst_ref=dst,
            send_sem=ring_sem.at[kind, u, w],
            recv_sem=(ag_sem, rs_sem)[kind].at[u, w, n],
            device_id=to,
            device_id_type=MESH,
        )

    barrier = pltpu.get_barrier_semaphore()
    peers = [dev(flip=True)]
    for flip in (False, True):
        peers += [dev(dz=1, flip=flip), dev(dz=-1, flip=flip)]
        peers += [dev(dg=1, flip=flip), dev(dg=-1, flip=flip)]
    for p in peers:
        pl.semaphore_signal(barrier, inc=1, device_id=p, device_id_type=MESH)

    def cols(base, width=D):
        return pl.ds(pl.multiple_of(base, D), width)

    def tables(b):
        pos = bp_ref[rows[b]] * BLK + lax.broadcasted_iota(jnp.int32, (BLK, D), 0)
        angle = pos.astype(F32) * fr_ref[...]
        cos_ref[b] = jnp.cos(angle)
        lane = lax.broadcasted_iota(jnp.int32, (BLK, D), 1)
        sin_ref[b] = jnp.where(lane < D // 2, -1.0, 1.0) * jnp.sin(angle)

    row0 = g * GB + 2 * z
    first = (g - 1) * GB
    rows = (row0 + other, row0 + c)
    loads[2].wait()
    loads[3].wait()
    tables(1)
    cos_own, sin_own = cos_ref[1], sin_ref[1]
    loads[5].wait()
    loads[6].wait()

    def rot(x, cs, sn):
        return x * cs + pltpu.roll(x, D // 2, 1) * sn

    def slot(grp, zc, pb):
        return grp * GB + 2 * zc + blk[pb]

    for u in range(2):
        for w in range(2):
            for pb in range(2):
                at = cols((blk[pb] * 2 + u) * D)
                if w == 0:
                    x = rot(k_ref[:, at].astype(F32), cos_own, sin_own).astype(BF)
                else:
                    x = v_ref[:, at]
                if pb == 0:
                    kvs[u][w][slot(1, z, 0)] = x
                else:
                    ks[u, w] = x
    loads[0].wait()
    loads[1].wait()
    pl.semaphore_wait(barrier, len(peers))

    def kv_chip(u, w, pb):
        return copy(ks.at[u, w], kvs[u][w].at[slot(1, z, pb)], kv_sem, (u, w), dev(flip=True))

    def x_copy(u, which):
        src = q_send.at[:, u * QW : (u + 1) * QW]
        if which == 0:
            src = do_ref.at[:, cols(other * HALF + u * QW, QW)]
        dst = (do_par, q_par)[which].at[:, u * QW : (u + 1) * QW]
        return copy(src, dst, x_sem, (which, u), dev(flip=True))

    def ag_copy(u, w, pb, grp, dr, d, arrived):
        p = kvs[u][w].at[slot(grp, at_z(-steps[dr] * (d if arrived else d - 1)), pb)]
        return ring_copy(p, p, 0, u, w, (pb, grp, dr, d), dev(dz=steps[dr]))

    def ay_copy(u, w, pb, k):
        src = kvs[u][w].at[slot(1, at_z(k), pb)]
        dst = kvs[u][w].at[slot(0, at_z(k), pb)]
        return ring_copy(src, dst, 0, u, w, (pb, k), dev(dg=1))

    def ev_begin(u, w, pb):
        if pb == 1:
            kv_chip(u, w, 1).wait_recv()
        ay_copy(u, w, pb, 0).start()
        for dr in range(2):
            ag_copy(u, w, pb, 1, dr, 1, False).start()

    def ev_own(u, w, pb, dr, k):
        ag_copy(u, w, pb, 1, dr, k, True).wait_recv()
        if k < far_of(dr, pb):
            ag_copy(u, w, pb, 1, dr, k + 1, False).start()
        if k <= reach[u]:
            ay_copy(u, w, pb, -steps[dr] * k).start()

    def ev_prev0(u, w, pb):
        ay_copy(u, w, pb, 0).wait_recv()
        if reach[u] < 1:
            for dr in range(2):
                ag_copy(u, w, pb, 0, dr, 1, False).start()

    def ev_prev(u, w, pb, dr, k):
        if k <= reach[u]:
            ay_copy(u, w, pb, -steps[dr] * k).wait_recv()
        else:
            ag_copy(u, w, pb, 0, dr, k, True).wait_recv()
        if reach[u] < k + 1 <= far_of(dr, pb):
            ag_copy(u, w, pb, 0, dr, k + 1, False).start()

    def q_rope(u):
        if u == 0:
            loads[4].wait()
        for mine in (False, True):
            base = (c if mine else other) * HALF + u * QW
            dst = q_own if mine else q_send
            for h in range(8):
                x = q_ref[:, cols(base + h * D)].astype(F32)
                x = rot(x, cos_own, sin_own) * (SCALE * LOG2E)
                dst[:, u * QW + h * D : u * QW + (h + 1) * D] = x.astype(BF)
            if not mine:
                start(x_copy(u, 1))

    def invert(kb, carry):
        for b in range(2):
            found = jnp.int32(KB)
            for j in range(KB):
                hit = (kb_ref[j, rows[b]] - first == kb) & (j < kc_ref[rows[b]])
                found = jnp.where(hit, j, found)
            inv[b, kb] = found
        return carry

    def invert_all():
        for b in range(2):
            for u in range(2):
                for w in range(2):
                    pts[u][w][b, KB] = jnp.zeros((D, BLK), BF)
        lax.fori_loop(0, 2 * GB, invert, 0)

    def set_ones():
        for b in range(2):
            vg[b, :, D:] = jnp.ones((NK, D), BF)

    rr = lax.broadcasted_iota(jnp.int32, (ROWS, BLK), 0) & (BLK - 1)
    cc = lax.broadcasted_iota(jnp.int32, (ROWS, BLK), 1)

    def listed(b, j):
        return jnp.clip(kb_ref[j, rows[b]] - first, 0, 2 * GB - 1)

    def head_rows(half):
        return slice(half * ROWS, (half + 1) * ROWS), [half * 4 + x for x in range(4)]

    def scores(u, b, half):
        if half == 0:
            if b == 0:
                x_copy(u, 1).wait_recv()
            for j in range(KB):
                kg[b, j * BLK : (j + 1) * BLK, :] = kvs[u][0][listed(b, j)]
        count = kc_ref[rows[b]]
        r, heads = head_rows(half)
        src_q = q_par if b == 0 else q_own
        q = jnp.concatenate(
            [src_q[:, u * QW + h * D : u * QW + (h + 1) * D] for h in heads], axis=0
        )
        q_t[b, :, r] = q.T
        mx = None
        for n in range(NK // KW):
            s = nt(q, kg[b, n * KW : (n + 1) * KW, :])
            for t in range(KW // BLK):
                j = n * (KW // BLK) + t
                st = s[:, t * BLK : (t + 1) * BLK]
                if j == 0:
                    st = jnp.where((cc <= rr) & (j < count), st, -1e30)
                else:
                    st = jnp.where(j < count, st, -1e30)
                s_scr[:, j * BLK : (j + 1) * BLK] = st
                mx = st if mx is None else jnp.maximum(mx, st)
        m = jnp.max(mx, axis=1, keepdims=True)
        for j in range(KB):
            ks_ = slice(j * BLK, (j + 1) * BLK)
            e_scr[b, r, ks_] = jnp.exp2(s_scr[:, ks_] - m).astype(BF)

    def attend(u, b, half):
        if half == 0:
            if b == 0:
                x_copy(u, 0).wait_recv()
            for j in range(KB):
                vg[b, j * BLK : (j + 1) * BLK, 0:D] = kvs[u][1][listed(b, j)]
        r, heads = head_rows(half)
        ox = nn(e_scr[b, r, :], vg[b])
        norm = 1.0 / ox[:, D:]
        o = ox[:, :D] * norm
        if b == 0:
            gr = [do_par[:, u * QW + h * D : u * QW + (h + 1) * D] for h in heads]
        else:
            gr = [do_ref[:, cols(c * HALF + u * QW + h * D)] for h in heads]
        gs = (jnp.concatenate(gr, axis=0).astype(F32) * norm).astype(BF)
        do_t[b, :, r] = gs.T
        g_scr[b, r, :] = gs
        delta = jnp.sum(gs.astype(F32) * o, axis=1, keepdims=True)
        dl_scr[b, r, :] = jnp.broadcast_to(delta, (ROWS, D))
        for x, h in enumerate(heads):
            oh = o[x * BLK : (x + 1) * BLK].astype(BF)
            if b == 0:
                o_scr[:, u * QW + h * D : u * QW + (h + 1) * D] = oh
            else:
                out_ref[:, cols(c * HALF + u * QW + h * D)] = oh

    def back(u, b, half):
        r, heads = head_rows(half)
        gs = g_scr[b, r, :]
        delta = dl_scr[b, r, :]
        for n in range(NK // KW):
            dp = nt(gs, vg[b, n * KW : (n + 1) * KW, 0:D])
            for t in range(KW // BLK):
                ks_ = slice(n * KW + t * BLK, n * KW + (t + 1) * BLK)
                x = e_scr[b, r, ks_].astype(F32) * (dp[:, t * BLK : (t + 1) * BLK] - delta)
                ds_scr[b, r, ks_] = x.astype(BF)
        dq = nn(ds_scr[b, r, :], kg[b])
        cs, sn = cos_ref[b] * SCALE, sin_ref[b] * -SCALE
        for x, h in enumerate(heads):
            dh = rot(dq[x * BLK : (x + 1) * BLK], cs, sn).astype(BF)
            if b == 0:
                dq_scr[:, u * QW + h * D : u * QW + (h + 1) * D] = dh
            else:
                qg_ref[:, cols(c * HALF + u * QW + h * D)] = dh

    def o_copy(u, which, core):
        src, dst = ((o_scr, out_ref), (dq_scr, qg_ref))[which]
        return copy(
            src.at[:, u * QW : (u + 1) * QW],
            dst.at[:, cols(core * HALF + u * QW, QW)],
            o_sem,
            (u, which),
            dev(flip=True),
        )

    def grads(w, u, b):
        if b == 0:
            start(o_copy(u, 1 - w, c))
        lhs, rhs = ((q_t, ds_scr), (do_t, e_scr))[w]
        for n in range(NK // KW):
            x = nn(lhs[b], rhs[b, :, n * KW : (n + 1) * KW])
            for t in range(KW // BLK):
                j = n * (KW // BLK) + t
                pts[u][w][b, j] = x[:, t * BLK : (t + 1) * BLK].astype(BF)

    def key_grads(u, b):
        grads(0, u, b)

    def value_grads(u, b):
        grads(1, u, b)

    def do_send(u):
        if u == 0:
            loads[7].wait()
        start(x_copy(u, 0))

    def term(u, w, grp, zc, pb):
        at = slot(grp, zc, pb)
        p = pts[u][w]
        return p[0, inv[0, at]].astype(F32) + p[1, inv[1, at]].astype(F32)

    def rs_copy(u, w, pb, grp, dr, k, arrived=False):
        if k == far_of(dr, pb) and not arrived:
            src = sb.at[u, w, pb, grp, dr]
        else:
            src = rbs[u][w].at[pb, grp, dr, min(k, FAR - 1)]
        dst = rbs[u][w].at[pb, grp, dr, k - 1]
        to = dev(dz=steps[dr], flip=grp == 1 and pb == 1 and k == 1)
        return ring_copy(src, dst, 1, u, w, (pb, grp, dr, k), to)

    def ry_copy(u, w, pb, dr, k):
        at = k if dr == 0 else -k
        src = rbs[u][w].at[pb, 0, dr, k]
        to = dev(dg=-1, flip=pb == 1 and k == 0)
        return ring_copy(src, yb.at[u, w, pb, at + MAX_REACH], 1, u, w, (pb, at), to)

    def ev_sum_own(u, w, pb, dr, k):
        x = term(u, w, 1, at_z(steps[dr] * k), pb)
        dst = sb.at[u, w, pb, 1, dr]
        if k < far_of(dr, pb):
            rs_copy(u, w, pb, 1, dr, k + 1, True).wait_recv()
            dst = rbs[u][w].at[pb, 1, dr, k]
            x = x + dst[...].astype(F32)
        if k <= reach_r[u]:
            ry_copy(u, w, pb, dr, k).wait_recv()
            x = x + yb[u, w, pb, (k if dr == 0 else -k) + MAX_REACH].astype(F32)
        dst[...] = x.astype(BF)
        rs_copy(u, w, pb, 1, dr, k).start()

    def ev_sum_prev(u, w, pb, dr, k):
        x = term(u, w, 0, at_z(steps[dr] * k), pb)
        dst = rbs[u][w].at[pb, 0, dr, min(k, FAR - 1)]
        if k >= reach_r[u] and k < far_of(dr, pb):
            rs_copy(u, w, pb, 0, dr, k + 1, True).wait_recv()
            x = x + dst[...].astype(F32)
        elif k > reach_r[u]:
            dst = sb.at[u, w, pb, 0, dr]
        dst[...] = x.astype(BF)
        if k > reach_r[u]:
            rs_copy(u, w, pb, 0, dr, k).start()
        else:
            ry_copy(u, w, pb, dr, k).start()

    def ev_sum_prev0(u, w, pb):
        x = term(u, w, 0, z, pb)
        if reach_r[u] == 0:
            for dr in range(2):
                rs_copy(u, w, pb, 0, dr, 1, True).wait_recv()
                x = x + rbs[u][w][pb, 0, dr, 0].astype(F32)
        rbs[u][w][pb, 0, 0, 0] = x.astype(BF)
        ry_copy(u, w, pb, 0, 0).start()

    def f_copy(u, w):
        return copy(f_s.at[u, w], f_r.at[u, w], f_sem, (u, w), dev(flip=True))

    def ev_sum_home(u, w, pb):
        if pb == 0:
            x = term(u, w, 1, z, 0)
        else:
            f_copy(u, w).wait_recv()
            x = f_r[u, w]
        for dr in range(2):
            rs_copy(u, w, pb, 1, dr, 1, True).wait_recv()
            x = x + rbs[u][w][pb, 1, dr, 0].astype(F32)
        ry_copy(u, w, pb, 0, 0).wait_recv()
        x = x + yb[u, w, pb, MAX_REACH].astype(F32)
        finish(u, w, blk[pb], x)

    def ev_hand_over(u, w, pb):
        if pb == 1:
            f_s[u, w] = term(u, w, 1, z, 1)
            start(f_copy(u, w))

    def finish(u, w, core, x):
        at = cols((core * 2 + u) * D)
        x = x.T
        if w == 0:
            x = rot(x * (1.0 / LOG2E), cos_own, -sin_own)
            kgr_ref[:, at] = x.astype(BF)
        else:
            vgr_ref[:, at] = x.astype(BF)

    for u in range(2):
        for w in range(2):
            start(kv_chip(u, w, 0))
    events = (
        (ev_begin, 3),
        (ev_own, 5),
        (ev_prev, 5),
        (ev_prev0, 3),
        (ev_sum_own, 5),
        (ev_sum_prev, 5),
        (ev_sum_prev0, 3),
        (ev_sum_home, 3),
        (ev_hand_over, 3),
        (scores, 3),
        (attend, 3),
        (back, 3),
        (key_grads, 2),
        (value_grads, 2),
        (q_rope, 1),
        (do_send, 1),
        (functools.partial(tables, 0), 0),
        (invert_all, 0),
        (set_ones, 0),
    )
    for item in ORDER:
        run, count = events[item // 100000]
        run(*[item // 10 ** (4 - i) % 10 for i in range(count)])
    for u in range(2):
        for which in range(2):
            o_copy(u, which, other).wait_recv()
    for d in sends:
        d.wait_send()
    for kind in range(2):
        for u in range(2):
            for w in range(2):
                assert len(places[kind, u, w]) == PIECES
                every = kvs[u][w].at[pl.ds(0, PIECES)]
                pltpu.make_async_remote_copy(
                    src_ref=every,
                    dst_ref=every,
                    send_sem=ring_sem.at[kind, u, w],
                    recv_sem=ag_sem.at[0, 0, 0],
                    device_id=dev(dz=1),
                    device_id_type=MESH,
                ).wait_send()


def scratch_groups(tok, n_blocks):
    V = pltpu.VMEM
    dma = pltpu.SemaphoreType.DMA
    sems = [dma((8,)), dma((2, 2, 2)), dma((2, 2, PIECES)), dma((2, 2, PIECES))]
    sems += [dma((2, 2))] * 8
    return [
        [V((2 * GB, BLK, D), BF)] * 4,
        [V((2, KB + 1, D, BLK), BF)] * 4,
        [V((2, 2, 2, FAR, D, BLK), BF)] * 4,
        [V((2, 2, BLK, D), BF)] + [V((tok, HALF), BF)] * 6,
        [
            V((2, 2, 2, 2, 2, D, BLK), BF),
            V((2, 2, 2, 2 * MAX_REACH + 1, D, BLK), BF),
            V((2, 2, D, BLK), F32),
            V((2, 2, D, BLK), F32),
        ],
        [
            pltpu.SMEM((KB, n_blocks), jnp.int32),
            pltpu.SMEM((n_blocks,), jnp.int32),
            pltpu.SMEM((n_blocks,), jnp.int32),
            V((1, D), F32),
            V((tok, HEADS * D), BF),
            V((tok, KV_HEADS * D), BF),
            V((tok, KV_HEADS * D), BF),
            V((tok, HEADS * D), BF),
            V((2, BLK, D), F32),
            V((2, BLK, D), F32),
        ],
        [
            V((2, NK, D), BF),
            V((2, NK, 2 * D), BF),
            V((ROWS, NK), F32),
            V((2, 8 * BLK, NK), BF),
            V((2, 8 * BLK, NK), BF),
            V((2, D, 8 * BLK), BF),
            V((2, D, 8 * BLK), BF),
            V((2, 8 * BLK, D), BF),
            V((2, 8 * BLK, D), F32),
            pltpu.SMEM((2, 2 * GB), jnp.int32),
        ],
        sems,
    ]


def split(refs):
    out, at = [], 0
    for n in [8, 4] + [len(x) for x in scratch_groups(BLK, 2 * GB)]:
        out.append(refs[at : at + n])
        at += n
    return out


def store(*refs):
    copies = [pltpu.make_async_copy(refs[i], refs[4 + i], refs[8].at[i]) for i in range(4)]
    for d in copies:
        d.start()
    for d in copies:
        d.wait()


def local(n_grp, n_seq, q, k, v, do, key_blocks, key_counts, block_position):
    vm = pl.BlockSpec(memory_space=pltpu.VMEM)
    hbm = pl.BlockSpec(memory_space=pltpu.HBM)
    scratch = [x for group in scratch_groups(q.shape[0], key_counts.shape[0]) for x in group]
    shapes = [jax.ShapeDtypeStruct(x.shape, BF) for x in (q, q, k, k)]
    operands = [
        pltpu.with_memory_space_constraint(x, pltpu.HBM)
        for x in (key_blocks.T, key_counts, block_position, jnp.asarray(FREQ), q, k, v, do)
    ]
    results = pl.pallas_call(
        functools.partial(kernel, n_grp, n_seq // 2, REACH, REACH_R),
        out_shape=shapes,
        in_specs=[hbm] * 8,
        out_specs=[vm] * 4,
        scratch_shapes=scratch,
        compiler_params=pltpu.CompilerParams(
            collective_id=0, has_side_effects=True, vmem_limit_bytes=48 * 2**20
        ),
    )(*operands)
    return pl.pallas_call(
        store,
        out_shape=shapes,
        in_specs=[pl.BlockSpec(memory_space=pl.ANY)] * 4,
        out_specs=[hbm] * 4,
        scratch_shapes=[pltpu.SemaphoreType.DMA((4,))],
        compiler_params=pltpu.CompilerParams(vmem_limit_bytes=2**20),
    )(*results)


def solution(mesh):
    rows = P(("grp", "seq"), None)
    return jax.shard_map(
        functools.partial(local, mesh.shape["grp"], mesh.shape["seq"]),
        mesh=mesh,
        in_specs=(rows, rows, rows, rows, P(), P(), P()),
        out_specs=(rows, rows, rows, rows),
        check_vma=False,
    )
```
